32 devices in a mesh: head: 4 (over y, x), space: 8 (over z, core).
Axes of the slice: x: 2, y: 2, z: 4, core: 2. Of those that a mesh axis runs over, the one named last changes fastest.
Arguments:
- features: bfloat16 [1024, 512, 256], P('space', 'head'), may hold values from -6 to 6
- stain_delta: float32 [256], replicated, may hold values from -0.4 to 0.4
- tissue: int32 [16, 8], P('space', 'head'), may hold values from 0 to 1, as said below
- reduce_weight: bfloat16 [256, 128], replicated, may hold values from -0.375 to 0.375
- spatial_weight: bfloat16 [3, 3, 128, 128], replicated, may hold values from -0.1875 to 0.1875
- expand_weight: bfloat16 [128, 512], replicated, may hold values from -0.5 to 0.5
- shortcut_weight: bfloat16 [256, 512], replicated, may hold values from -0.375 to 0.375
- attn_tanh: float32 [512, 256], replicated, may hold values from -1 to 1
- attn_sigm: float32 [512, 256], replicated, may hold values from -1 to 1
- attn_out: float32 [256], replicated, may hold values from -2 to 2
- classifier: float32 [512], replicated, may hold values from -0.75 to 0.75
- step_dir: int32 [256], replicated, may hold values from 0 to 1
Outputs:
- feature_grad: bfloat16 [1024, 512, 256], P('space', 'head')
- new_delta: float32 [256], replicated
The draws below stay inside these ranges and needn't reach their ends.
Inputs may be any that keep to these rules, and one draw needn't show every extreme that they name: The tile at the slide's first row and column holds tissue.
All inputs are finite; a program needn't handle non-finite values.
Results may differ from the reference program's by a relative error of at most 0.0065.
Values may be sent and summed in bfloat16 or wider, within the bound.
A program may use at most 128 MiB of HBM per device.

```python
import jax
import jax.numpy as jnp
from jax import lax

CIN = 256
MID = 128
COUT = 512
ATT = 256
TILE = 64
HGT = 1024
WID = 512
ALPHA = 1


def draw_tissue(key, part):
    marks = jax.random.randint(key, (HGT // TILE, WID // TILE), 0, 5)
    marks = jnp.where(marks >= 2, 1, 0).astype(jnp.int32)
    return marks.at[0, 0].set(1)


def gate_noise(key, salt):
    noise = jax.random.normal(jax.random.fold_in(key, salt), (COUT, ATT), jnp.float32)
    return jnp.clip(noise, -2.5, 2.5) * (8.0 / COUT) ** 0.5


def draw_attn_tanh(key, part):
    noise = gate_noise(key, 21)
    return noise


def draw_attn_sigm(key, part):
    noise = gate_noise(key, 22)
    return noise


def draw_attn_out(key, part):
    values = jnp.clip(jax.random.normal(jax.random.fold_in(key, 32), (ATT,), jnp.float32), -2.5, 2.5) * (16.0 / ATT) ** 0.5
    return values


def touch_ends(entries, key, low, top_value):
    spot = [jax.random.randint(jax.random.fold_in(key, axis), (), 0, length) for axis, length in enumerate(entries.shape)]
    widest = entries.shape.index(max(entries.shape))
    next_to = spot[:widest] + [(spot[widest] + 1) % entries.shape[widest]] + spot[widest + 1:]
    return entries.at[tuple(spot)].set(low).at[tuple(next_to)].set(top_value)


def level_of(own_key, extent, cuts, least, high):
    factor_of = 1.0
    for axis_at, parts in cuts:
        steps = jax.random.uniform(jax.random.fold_in(jax.random.fold_in(own_key, 6), axis_at), (parts,), jnp.float32, least / len(cuts), high / len(cuts))
        factor_of = factor_of * jnp.repeat(jnp.exp(steps), extent[axis_at] // parts).reshape((-1,) + (1,) * (len(extent) - 1 - axis_at))
    return factor_of


def scatter_about(own_key, dims, scale, most, split=(), held_as=jnp.bfloat16):
    loudness = level_of(own_key, dims, split, -0.22, 0.18) if split else 1.0
    entries = jax.random.normal(own_key, dims, jnp.float32) * scale * loudness
    return jnp.minimum(jnp.maximum(entries, -most), most).astype(held_as)


def setup_inputs(seed: int = 0) -> dict:
    splits = jax.random.split(jax.random.key(seed), 13)
    return {
        "features": scatter_about(splits[0], (HGT, WID, CIN), 1.0, 6.0, ((0, 8), (1, 4))),
        "stain_delta": jnp.clip(jax.random.uniform(splits[1], (CIN,), jnp.float32, -0.4, 0.4), -0.4, 0.4),
        "tissue": draw_tissue(jax.random.fold_in(splits[12], 71), 0),
        "reduce_weight": scatter_about(splits[3], (CIN, MID), CIN ** -0.5, 0.375),
        "spatial_weight": scatter_about(splits[4], (3, 3, MID, MID), (9 * MID) ** -0.5, 0.1875),
        "expand_weight": scatter_about(splits[5], (MID, COUT), MID ** -0.5, 0.5),
        "shortcut_weight": scatter_about(splits[6], (CIN, COUT), CIN ** -0.5, 0.375),
        "attn_tanh": draw_attn_tanh(jax.random.fold_in(splits[12], 71), 0),
        "attn_sigm": draw_attn_sigm(jax.random.fold_in(splits[12], 71), 0),
        "attn_out": draw_attn_out(jax.random.fold_in(splits[12], 71), 0),
        "classifier": scatter_about(splits[10], (COUT,), (COUT // 8) ** -0.5, 0.75, (), jnp.float32),
        "step_dir": touch_ends(jax.random.randint(splits[11], (CIN,), 0, 2), jax.random.fold_in(splits[11], 1), 0, 1).astype(jnp.int32),
    }


def silu_slope(value):
    sig = jax.nn.sigmoid(value)
    return sig * (1.0 + value * (1.0 - sig))

def reference(features, stain_delta, tissue, reduce_weight, spatial_weight, expand_weight, shortcut_weight, attn_tanh, attn_sigm, attn_out, classifier, step_dir):
    hp = lax.Precision.HIGHEST
    rows, cols, chan = features.shape
    mid = reduce_weight.shape[1]
    cout = expand_weight.shape[1]
    scale = 1.0 + stain_delta
    perturbed = (features.astype(jnp.float32) * scale).astype(jnp.bfloat16)
    reduce_pre = jnp.dot(perturbed.reshape(-1, chan), reduce_weight, preferred_element_type=jnp.float32).reshape(rows, cols, mid)
    reduced = jax.nn.silu(reduce_pre).astype(jnp.bfloat16)
    padded = jnp.pad(reduced, ((1, 0), (1, 0), (0, 0)))
    orow, ocol = (rows // 2, cols // 2)
    acc = jnp.zeros((orow * ocol, mid), jnp.float32)
    for a in range(3):
        for b in range(3):
            tap = padded[a:a + rows:2, b:b + cols:2].reshape(-1, mid)
            acc = acc + jnp.dot(tap, spatial_weight[a, b], preferred_element_type=jnp.float32)
    spatial = jax.nn.silu(acc).astype(jnp.bfloat16)
    short_in = perturbed[::2, ::2].reshape(-1, chan)
    preact = jnp.dot(spatial, expand_weight, preferred_element_type=jnp.float32) + jnp.dot(short_in, shortcut_weight, preferred_element_type=jnp.float32)
    block = jax.nn.silu(preact).reshape(orow, ocol, cout)
    half = TILE // 2
    embed = block.reshape(orow // half, half, ocol // half, half, cout).mean(axis=(1, 3))
    tiles_r, tiles_c = (embed.shape[0], embed.shape[1])
    flat = embed.reshape(-1, cout)
    tval = jnp.tanh(jnp.dot(flat, attn_tanh, precision=hp))
    gval = jax.nn.sigmoid(jnp.dot(flat, attn_sigm, precision=hp))
    score = jnp.dot(tval * gval, attn_out, precision=hp)
    live = tissue.reshape(-1) > 0
    top = jnp.max(jnp.where(live, score, -1e+30))
    weights = jnp.where(live, jnp.exp(score - top), 0.0)
    total = jnp.sum(weights)
    pooled = jnp.dot(weights, flat, precision=hp) / total
    prob = weights / total
    mean_logit = jnp.dot(pooled, classifier, precision=hp)
    dprob = jnp.dot(flat, classifier, precision=hp)
    dscore = prob * (dprob - mean_logit)
    datt = dscore[:, None] * attn_out[None, :]
    dtanh = datt * gval * (1.0 - tval * tval)
    dsigm = datt * tval * gval * (1.0 - gval)
    dembed = prob[:, None] * classifier[None, :] + jnp.dot(dtanh, attn_tanh.T, precision=hp) + jnp.dot(dsigm, attn_sigm.T, precision=hp)
    dembed = dembed.reshape(tiles_r, 1, tiles_c, 1, cout) / float(half * half)
    dblock = jnp.broadcast_to(dembed, (tiles_r, half, tiles_c, half, cout)).reshape(-1, cout)
    dpre = (dblock * silu_slope(preact)).astype(jnp.bfloat16)
    dspatial = (jnp.dot(dpre, expand_weight.T, preferred_element_type=jnp.float32) * silu_slope(acc)).astype(jnp.bfloat16)
    dshort = jnp.dot(dpre, shortcut_weight.T, preferred_element_type=jnp.float32).reshape(orow, ocol, chan)
    dpad = jnp.zeros((rows + 1, cols + 1, mid), jnp.float32)
    for a in range(3):
        for b in range(3):
            part = jnp.dot(dspatial, spatial_weight[a, b].T, preferred_element_type=jnp.float32).reshape(orow, ocol, mid)
            dpad = dpad.at[a:a + rows:2, b:b + cols:2].add(part)
    dreduced = (dpad[1:, 1:] * silu_slope(reduce_pre)).astype(jnp.bfloat16)
    dinput = jnp.dot(dreduced.reshape(-1, mid), reduce_weight.T, preferred_element_type=jnp.float32).reshape(rows, cols, chan)
    dinput = dinput.at[::2, ::2].add(dshort)
    feature_grad = (dinput * scale).astype(jnp.bfloat16)
    ddelta = lax.optimization_barrier(jnp.sum(dinput * features.astype(jnp.float32), axis=(0, 1)))
    norm_size = jnp.sqrt(jnp.mean(ddelta * ddelta) + 1e-06)
    direction = (2 * step_dir - 1).astype(jnp.float32)
    new_delta = stain_delta + direction * float(ALPHA) * ddelta / norm_size
    return (feature_grad, new_delta)
```

```python
import functools

import jax
import jax.numpy as jnp
from jax import lax
from jax.experimental import pallas as pl
from jax.experimental.pallas import tpu as pltpu
from jax.sharding import PartitionSpec as P

TILE = 64
ALPHA = 1
BLOCK = 32
SUB = 8
F32 = jnp.float32
BF16 = jnp.bfloat16
MESH = pl.DeviceIdType.MESH
AXES = ("head", "space")


def sigm(value):
    return 0.5 + 0.5 * jnp.tanh(0.5 * value)


def silu_pair(h):
    t = jnp.tanh(h)
    u = 1.0 + t
    act = h * u
    return act, u + act * (1.0 - t)


def dot(a, b):
    return jnp.dot(a, b, preferred_element_type=F32)


def dot_t(a, b):
    return lax.dot_general(a, b, (((1,), (1,)), ((), ())), preferred_element_type=F32)


def column(row, width):
    return jnp.transpose(jnp.broadcast_to(row, (width, row.shape[1])))


def split(value):
    high = value.astype(BF16)
    return high, (value - high.astype(F32)).astype(BF16)


def shifted(sizes, a, b):
    return (
        lax.rem(lax.axis_index(AXES[0]) + sizes[0] + a, sizes[0]),
        lax.rem(lax.axis_index(AXES[1]) + sizes[1] + b, sizes[1]),
    )


def others(sizes):
    return [shifted(sizes, a, b) for a in range(sizes[0]) for b in range(sizes[1]) if a + b > 0]


def remote(source, target, send, recv, device):
    return pltpu.make_async_remote_copy(
        src_ref=source, dst_ref=target, send_sem=send, recv_sem=recv, device_id=device, device_id_type=MESH
    )


def edge_copies(edges, landed, send, recv, spans, targets):
    return [
        remote(edges.at[pl.ds(source, size)], landed.at[pl.ds(place, size)], send.at[k], recv.at[k], targets[k])
        for k, (source, size, place) in enumerate(spans)
    ]


def whole_kernel(
    sizes, x_ref, delta_ref, dir_ref, tissue_ref, wr_ref, sp_ref, we_ref, ws_ref, at_ref, as_ref, ao_ref, cls_ref,
    out_ref, delta_out,
    xv, red, s1, s2, s3, dsx, drs, slo, shi, wrh, wph, wf, wb, gate, ghigh, glow, sums, col2, col3, carry2, carry3,
    rowbuf, colbuf, up, left, edges1, landed1, edges2, landed2, mine1, got1, mine2, got2, dembed_ref, total_ref,
    x_sem, in_sem, es1, er1, es2, er2, xs1, xr1, xs2, xr2,
):
    rows, cols, chan = xv.shape
    mid, cout = we_ref.shape
    orow, ocol = rows // 2, cols // 2
    half = TILE // 2
    tiles_r, tiles_c = tissue_ref.shape
    slots = sums.shape[0]
    steps = rows // BLOCK
    ob = BLOCK // 2
    att = ao_ref.shape[1]
    everyone = others(sizes)

    row_in = pltpu.make_async_copy(x_ref.at[pl.ds(rows - 1, 1)], rowbuf, in_sem.at[0])
    col_in = pltpu.make_async_copy(x_ref.at[:, pl.ds(cols - 2 * SUB, 2 * SUB), :], colbuf, in_sem.at[1])
    row_in.start()
    col_in.start()

    def chunk(k):
        return pltpu.make_async_copy(
            x_ref.at[pl.ds(k * BLOCK, BLOCK)], xv.at[pl.ds(k * BLOCK, BLOCK)], x_sem.at[k]
        )

    for k in range(steps):
        chunk(k).start()
    gate_in = [
        pltpu.make_async_copy(ref, gate.at[:, pl.ds(k * att, att)], in_sem.at[2 + k])
        for k, ref in enumerate((at_ref, as_ref))
    ]
    for copy in gate_in:
        copy.start()

    barrier = pltpu.get_barrier_semaphore()
    for device in everyone:
        pl.semaphore_signal(barrier, inc=1, device_id=device, device_id_type=MESH)

    wide = column(0.5 + 0.5 * delta_ref[...], mid)
    wrh[...] = (wr_ref[...].astype(F32) * wide).astype(BF16)
    wph[:mid, :] = (we_ref[...].astype(F32) * 0.5).astype(BF16)
    for k in range(cout // mid):
        at = slice(k * mid, (k + 1) * mid)
        wph[mid:, at] = (ws_ref[:, at].astype(F32) * wide).astype(BF16)
    none = jnp.zeros((mid, mid), BF16)
    for b in range(3):
        tap = [(sp_ref[a, b].astype(F32) * 0.5).astype(BF16) for a in range(3)]
        at = slice(b * mid, (b + 1) * mid)
        under = slice((3 + b) * mid, (4 + b) * mid)
        wf[at, :mid] = tap[1]
        wf[at, mid:] = none
        wf[under, :mid] = tap[2]
        wf[under, mid:] = tap[0]
        for k, a in enumerate((1, 2, 0)):
            if b == 0:
                wb[(2 * k + 1) * mid : (2 * k + 2) * mid, mid:] = tap[a]
                wb[2 * k * mid : (2 * k + 1) * mid, mid:] = none
            else:
                wb[(2 * k + b - 1) * mid : (2 * k + b) * mid, :mid] = tap[a]

    row_in.wait()
    col_in.wait()
    col = colbuf[:, SUB:, :].astype(F32)[:, SUB - 1, :].astype(BF16)
    edge, _ = silu_pair(dot(jnp.concatenate([rowbuf[0], col], axis=0), wrh[...]))
    edges1[...] = edge.astype(BF16)
    copies1 = edge_copies(
        edges1, landed1, es1, er1,
        ((0, cols, 0), (cols, rows, cols), (cols - 2 * SUB, 2 * SUB, cols + rows)),
        (shifted(sizes, 0, 1), shifted(sizes, 1, 0), shifted(sizes, 1, 1)),
    )

    def reduce_block(k):
        chunk(k).wait()
        at = pl.ds(k * BLOCK, BLOCK)
        act, slope = silu_pair(dot(xv[at].reshape(BLOCK * cols, chan), wrh[...]))
        s1[at] = slope.reshape(BLOCK, cols, mid).astype(s1.dtype)
        red[at, SUB:, :] = act.reshape(BLOCK, cols, mid)

    reduce_block(0)
    pl.semaphore_wait(barrier, len(everyone))
    for copy in copies1:
        copy.start()
    for k in range(1, steps):
        reduce_block(k)
    for copy in gate_in:
        copy.wait()
    high, low = split(gate[...])
    ghigh[...] = high
    glow[...] = low
    for copy in copies1:
        copy.wait()
    above = jnp.where(lax.axis_index("space") > 0, 1.0, 0.0)
    beside = jnp.where(lax.axis_index("head") > 0, 1.0, 0.0)
    up[0:SUB, :] = landed1[cols + rows :, :].astype(F32)[SUB:] * (above * beside)
    up[SUB:, :] = landed1[0:cols, :].astype(F32) * above
    left[...] = landed1[cols : cols + rows, :].astype(F32) * beside
    for r in range(rows):
        red[r, SUB - 1 : SUB, :] = left[r : r + 1, :]
    sums[...] = jnp.zeros_like(sums)

    def taps_of(source):
        return [source[pl.ds(SUB - 1 + b, ocol, stride=2), :].astype(BF16) for b in range(3)]

    carry2[...] = dot(jnp.concatenate(taps_of(up), axis=1), wf[3 * mid :, mid:])

    def conv_block(k, none):
        first = pl.multiple_of(k * BLOCK, BLOCK)
        lines = [
            jnp.concatenate(taps_of(red.at[first + 2 * i]) + taps_of(red.at[first + 2 * i + 1]), axis=1)
            for i in range(ob)
        ]
        y = dot(jnp.concatenate(lines, axis=0), wf[...])
        later = y[:, mid:]
        now = y[:, :mid] + jnp.concatenate([carry2[...], later[: (ob - 1) * ocol]], axis=0)
        carry2[...] = later[(ob - 1) * ocol :]
        act, slope = silu_pair(now)
        slope = slope.reshape(ob, ocol, mid)
        at = pl.ds(pl.multiple_of(k * ob, ob), ob)
        s2[at] = slope.astype(s2.dtype)
        col2[at, :] = slope[:, 0, :]
        short = []
        for i in range(ob):
            slo[i] = xv[first + 2 * i, :, : chan // 2].astype(F32)
            shi[i] = xv[first + 2 * i, :, chan // 2 :].astype(F32)
        for i in range(ob):
            short.append(
                jnp.concatenate(
                    [room.at[i][pl.ds(0, ocol, stride=2), :].astype(BF16) for room in (slo, shi)], axis=1
                )
            )
        act, slope = silu_pair(
            dot(jnp.concatenate([act.astype(BF16), jnp.concatenate(short, axis=0)], axis=1), wph[...])
        )
        slope = slope.reshape(ob, ocol, cout)
        s3[at] = slope.astype(s3.dtype)
        col3[at, :] = slope[:, 0, :]
        cells = jnp.sum(act.reshape(ob, tiles_c, half // SUB, SUB, cout), axis=(0, 2))
        trow = (k * ob) // half
        for c in range(tiles_c):
            slot = trow * tiles_c + c
            sums[slot] = sums[slot] + cells[c]
        return none

    lax.fori_loop(0, steps, conv_block, 0)

    ao, cls = ao_ref[...], cls_ref[...]
    embed = jnp.sum(sums[...], axis=1) * (1.0 / (half * half))
    high, low = split(embed)
    first = dot(jnp.concatenate([high, low], axis=0), ghigh[...])
    gates = first[:slots] + first[slots:] + dot(high, glow[...])
    tval = jnp.tanh(gates[:, :att])
    gval = sigm(gates[:, att:])
    score = jnp.sum(tval * gval * ao, axis=1, keepdims=True)
    value = jnp.sum(embed * cls, axis=1, keepdims=True)
    slot = lax.broadcasted_iota(jnp.int32, (slots, 128), 0)
    marks = jnp.zeros(slot.shape, jnp.int32)
    for r in range(tiles_r):
        for c in range(tiles_c):
            mark = jnp.broadcast_to(tissue_ref[r : r + 1, c : c + 1], slot.shape)
            marks = jnp.where(slot == r * tiles_c + c, mark, marks)
    live = marks[:, 0:1] > 0
    top = jnp.max(jnp.where(live, score, -1e30), axis=0, keepdims=True)
    weight = jnp.where(live, jnp.exp(score - top), 0.0)
    lane = lax.broadcasted_iota(jnp.int32, (1, 128), 1)
    payload = jnp.where(
        lane == 0, top,
        jnp.where(
            lane == 1, jnp.sum(weight, axis=0, keepdims=True), jnp.sum(weight * value, axis=0, keepdims=True)
        ),
    )
    mine1[...] = payload
    got1[0] = payload
    copies = [remote(mine1, got1.at[k + 1], xs1.at[k], xr1.at[k], device) for k, device in enumerate(everyone)]
    for copy in copies:
        copy.start()
    dtanh = ao * gval * (1.0 - tval * tval)
    dsigm = ao * tval * gval * (1.0 - gval)
    high, low = split(jnp.concatenate([dtanh, dsigm], axis=1))
    first = dot_t(jnp.concatenate([high, low], axis=0), ghigh[...])
    slant = first[:slots] + first[slots:] + dot_t(high, glow[...])
    for copy in copies:
        copy.wait()
    every = got1[...]
    best = jnp.max(every, axis=0)[:, 0:1]
    factor = jnp.exp(every[:, :, 0:1] - best[None])
    both = jnp.sum(every * factor, axis=0)
    total = both[:, 1:2]
    prob = jnp.where(live, jnp.exp(score - best), 0.0) / total
    gap = value - both[:, 2:3] / total
    dembed = prob * (cls + gap * slant) * (1.0 / (half * half))
    dembed_ref[...] = dembed

    def spread_rows(tiles):
        return jnp.concatenate([jnp.broadcast_to(dembed[t : t + 1], (half, cout)) for t in tiles], axis=0)

    line = jnp.concatenate([s3[0].astype(F32) * spread_rows(range(tiles_c)),
                            col3[...] * spread_rows(range(0, tiles_r * tiles_c, tiles_c))], axis=0).astype(BF16)
    line = dot_t(line, wph[:mid, :]) * jnp.concatenate([s2[0].astype(F32), col2[...]], axis=0)
    edges2[...] = line.astype(BF16)
    copies2 = edge_copies(
        edges2, landed2, es2, er2,
        ((0, ocol, 0), (ocol, orow, ocol), (0, 2 * SUB, ocol + orow)),
        (shifted(sizes, 0, -1), shifted(sizes, -1, 0), shifted(sizes, -1, -1)),
    )
    for copy in copies2:
        copy.start()

    def spatial_back(k, none):
        at = pl.ds(pl.multiple_of(k * ob, ob), ob)
        trow = (k * ob) // half
        spread = jnp.concatenate(
            [jnp.broadcast_to(dembed_ref[pl.ds(trow * tiles_c + c, 1), :], (half, cout)) for c in range(tiles_c)],
            axis=0,
        )
        dpre = (s3[at].astype(F32) * spread[None]).astype(BF16).reshape(ob * ocol, cout)
        both = dot_t(dpre, wph[...])
        dsx[at, 0:ocol, :] = both[:, :mid].reshape(ob, ocol, mid) * s2[at].astype(F32)
        for i in range(ob):
            line = both[i * ocol : (i + 1) * ocol]
            for c in range(2):
                room = red.at[pl.multiple_of(k * BLOCK, BLOCK) + 2 * i + c]
                room[pl.ds(0, ocol, stride=2), :] = line[:, mid + c * (chan // 2) : mid + (c + 1) * (chan // 2)]
                room[pl.ds(1, ocol, stride=2), :] = jnp.zeros((ocol, mid), F32)
        return none

    lax.fori_loop(0, steps, spatial_back, 0)
    for copy in copies2:
        copy.wait()
    below = jnp.where(lax.axis_index("space") < sizes[1] - 1, 1.0, 0.0)
    beside = jnp.where(lax.axis_index("head") < sizes[0] - 1, 1.0, 0.0)
    dsx[orow, 0:ocol, :] = landed2[0:ocol, :].astype(F32) * below
    dsx[orow, ocol:, :] = landed2[ocol + orow :, :].astype(F32)[:SUB] * (below * beside)
    left[0:orow, :] = landed2[ocol : ocol + orow, :].astype(F32) * beside
    for r in range(orow):
        dsx[r, ocol : ocol + 1, :] = left[r : r + 1, :]

    def pair(i):
        return jnp.concatenate([dsx[i, 0:ocol, :], dsx[i, 1 : ocol + 1, :]], axis=1).astype(BF16)

    carry3[...] = dot_t(pair(orow), wb[4 * mid :, :])
    total_ref[...] = jnp.zeros_like(total_ref)

    def reduced_back(step, none):
        k = steps - 1 - step
        first = pl.multiple_of(k * BLOCK, BLOCK)
        y = dot_t(jnp.concatenate([pair(k * ob + i) for i in range(ob)], axis=0), wb[...])
        for i in range(ob):
            at = slice(i * ocol, (i + 1) * ocol)
            below = carry3[...] if i == ob - 1 else y[(i + 1) * ocol : (i + 2) * ocol, 4 * mid :]
            odd = y[at, 2 * mid : 4 * mid] + below
            for dj in range(2):
                side = slice(dj * mid, (dj + 1) * mid)
                drs[2 * i, pl.ds(dj, ocol, stride=2), :] = y[at, side]
                drs[2 * i + 1, pl.ds(dj, ocol, stride=2), :] = odd[:, side]
        carry3[...] = y[0:ocol, 4 * mid :]
        dred = (drs[...] * s1[pl.ds(first, BLOCK)].astype(F32)).astype(BF16)
        dinput = dot_t(dred.reshape(BLOCK * cols, mid), wrh[...]).reshape(BLOCK, cols, chan)
        total = jnp.zeros((SUB, chan), F32)
        for r in range(BLOCK):
            value = dinput[r]
            if r % 2 == 0:
                value = value + jnp.concatenate([red[first + r, 0:cols, :], red[first + r + 1, 0:cols, :]], axis=1)
            out_ref[first + r] = value.astype(BF16)
            total = total + jnp.sum((value * xv[first + r].astype(F32)).reshape(cols // SUB, SUB, chan), axis=0)
        total_ref[...] += total
        return none

    lax.fori_loop(0, steps, reduced_back, 0)

    part = jnp.sum(total_ref[...], axis=0, keepdims=True)
    lines = chan // 128
    part = jnp.concatenate([part[:, k * 128 : (k + 1) * 128] for k in range(lines)], axis=0)
    mine2[...] = part
    got2[0] = part
    copies = [remote(mine2, got2.at[k + 1], xs2.at[k], xr2.at[k], device) for k, device in enumerate(everyone)]
    for copy in copies:
        copy.start()
    for copy in copies:
        copy.wait()
    part = jnp.sum(got2[...], axis=0)
    delta = delta_ref[...]
    ddelta = jnp.concatenate([part[k : k + 1] for k in range(lines)], axis=1) / (1.0 + delta)
    norm = jnp.sqrt(jnp.sum(ddelta * ddelta, axis=1, keepdims=True) * (1.0 / chan) + 1e-06)
    delta_out[...] = delta + (2 * dir_ref[...] - 1).astype(F32) * float(ALPHA) * ddelta / norm


def leave_kernel(v_ref, out_ref, sem):
    n = sem.shape[0]
    size = v_ref.shape[0] // n
    copies = [
        pltpu.make_async_copy(v_ref.at[pl.ds(k * size, size)], out_ref.at[pl.ds(k * size, size)], sem.at[k])
        for k in range(n)
    ]
    for copy in copies:
        copy.start()
    for copy in copies:
        copy.wait()


def shards(
    features, stain_delta, tissue, reduce_weight, spatial_weight, expand_weight, shortcut_weight, attn_tanh, attn_sigm,
    attn_out, classifier, step_dir,
):
    rows, cols, chan = features.shape
    mid = reduce_weight.shape[1]
    cout = expand_weight.shape[1]
    att = attn_out.shape[0]
    tiles_r, tiles_c = tissue.shape
    slots = -(-tiles_r * tiles_c // SUB) * SUB
    orow, ocol = rows // 2, cols // 2
    sizes = tuple(lax.axis_size(axis) for axis in AXES)
    n = sizes[0] * sizes[1]
    steps = rows // BLOCK
    ob = BLOCK // 2
    vmem = pl.BlockSpec(memory_space=pltpu.VMEM)
    hbm = pl.BlockSpec(memory_space=pl.ANY)
    V, D = pltpu.VMEM, pltpu.SemaphoreType.DMA

    grad, new_delta = pl.pallas_call(
        functools.partial(whole_kernel, sizes),
        out_shape=(OUT_SPACE((rows, cols, chan), BF16), jax.ShapeDtypeStruct((1, chan), F32)),
        in_specs=[hbm, vmem, vmem, vmem, vmem, vmem, vmem, vmem, hbm, hbm, vmem, vmem],
        out_specs=(vmem, vmem),
        scratch_shapes=[
            V((rows, cols, chan), BF16),
            V((rows, cols + SUB, mid), F32),
            V((rows, cols, mid), F32),
            V((orow, ocol, mid), F32),
            V((orow, ocol, cout), F32),
            V((orow + 1, ocol + SUB, mid), F32),
            V((BLOCK, cols, mid), F32),
            V((ob, cols, chan // 2), F32),
            V((ob, cols, chan // 2), F32),
            V((chan, mid), BF16),
            V((mid + chan, cout), BF16),
            V((6 * mid, 2 * mid), BF16),
            V((6 * mid, 2 * mid), BF16),
            V((cout, 2 * att), F32),
            V((cout, 2 * att), BF16),
            V((cout, 2 * att), BF16),
            V((slots, SUB, cout), F32),
            V((orow, mid), F32),
            V((orow, cout), F32),
            V((ocol, mid), F32),
            V((ocol, 2 * mid), F32),
            V((1, cols, chan), BF16),
            V((rows, 2 * SUB, chan), BF16),
            V((cols + SUB, mid), F32),
            V((rows, mid), F32),
            V((cols + rows, mid), BF16),
            V((cols + rows + 2 * SUB, mid), BF16),
            V((ocol + orow, mid), BF16),
            V((ocol + orow + 2 * SUB, mid), BF16),
            V((1, 128), F32),
            V((n, 1, 128), F32),
            V((chan // 128, 128), F32),
            V((n, chan // 128, 128), F32),
            V((slots, cout), F32),
            V((SUB, chan), F32),
            D((steps,)),
            D((4,)),
            D((3,)),
            D((3,)),
            D((3,)),
            D((3,)),
            D((n - 1,)),
            D((n - 1,)),
            D((n - 1,)),
            D((n - 1,)),
        ],
        compiler_params=pltpu.CompilerParams(
            vmem_limit_bytes=52 * 1024 * 1024, collective_id=0, has_side_effects=True
        ),
        name="slide",
    )(
        features, stain_delta[None, :], step_dir[None, :], tissue, reduce_weight, spatial_weight, expand_weight,
        shortcut_weight, attn_tanh, attn_sigm, attn_out[None, :], classifier[None, :],
    )
    feature_grad = pl.pallas_call(
        leave_kernel,
        out_shape=jax.ShapeDtypeStruct((rows, cols, chan), BF16),
        in_specs=[vmem],
        out_specs=hbm,
        scratch_shapes=[D((4,))],
        compiler_params=pltpu.CompilerParams(vmem_limit_bytes=1024 * 1024),
        name="leave",
    )(grad)
    return (feature_grad, new_delta[0])


def OUT_SPACE(shape, dtype):
    return pltpu.VMEM(shape, dtype)


def solution(mesh):
    return jax.shard_map(
        shards,
        mesh=mesh,
        in_specs=(P("space", "head", None), P(), P("space", "head")) + (P(),) * 9,
        out_specs=(P("space", "head", None), P()),
        check_vma=False,
    )
```

```python
import functools

import jax
import jax.numpy as jnp
from jax import lax
from jax.experimental import pallas as pl
from jax.experimental.pallas import tpu as pltpu
from jax.sharding import PartitionSpec as P

TILE = 64
ALPHA = 1
BLOCK = 32
SUB = 8
PART = 8
LINES = 8
F32 = jnp.float32
BF16 = jnp.bfloat16
MESH = pl.DeviceIdType.MESH
AXES = ("head", "space")


def sigm(value):
    return 0.5 + 0.5 * jnp.tanh(0.5 * value)


def silu_pair(h):
    t = jnp.tanh(h)
    u = 1.0 + t
    act = h * u
    return act, u + act * (1.0 - t)


def dot(a, b):
    return jnp.dot(a, b, preferred_element_type=F32)


def dot_t(a, b):
    return lax.dot_general(a, b, (((1,), (1,)), ((), ())), preferred_element_type=F32)


def column(row, width):
    return jnp.transpose(jnp.broadcast_to(row, (width, row.shape[1])))


def split(value):
    high = value.astype(BF16)
    return high, (value - high.astype(F32)).astype(BF16)


def shifted(sizes, a, b):
    return (
        lax.rem(lax.axis_index(AXES[0]) + sizes[0] + a, sizes[0]),
        lax.rem(lax.axis_index(AXES[1]) + sizes[1] + b, sizes[1]),
    )


def others(sizes):
    return [shifted(sizes, a, b) for a in range(sizes[0]) for b in range(sizes[1]) if a + b > 0]


def remote(source, target, send, recv, device):
    return pltpu.make_async_remote_copy(
        src_ref=source, dst_ref=target, send_sem=send, recv_sem=recv, device_id=device, device_id_type=MESH
    )


def edge_copies(edges, landed, send, recv, spans, targets):
    return [
        remote(edges.at[pl.ds(source, size)], landed.at[pl.ds(place, size)], send.at[k], recv.at[k], targets[k])
        for k, (source, size, place) in enumerate(spans)
    ]


def whole_kernel(
    sizes, x_ref, delta_ref, dir_ref, tissue_ref, wr_ref, sp_ref, we_ref, ws_ref, at_ref, as_ref, ao_ref, cls_ref,
    out_ref, delta_out,
    xv, red, s1, s2, s3, dsx, drs, slo, shi, wrh, wph, wf, wb, gate, ghigh, glow, sums, col2, col3, carry2, carry3,
    rowbuf, colbuf, up, left, edges1, landed1, edges2, landed2, mine1, got1, mine2, got2, dembed_ref, total_ref,
    x_sem, in_sem, es1, er1, es2, er2, xs1, xr1, xs2, xr2,
):
    rows, cols, chan = xv.shape
    mid, cout = we_ref.shape
    orow, ocol = rows // 2, cols // 2
    half = TILE // 2
    tiles_r, tiles_c = tissue_ref.shape
    slots = sums.shape[0]
    steps = rows // BLOCK
    ob = BLOCK // 2
    att = ao_ref.shape[1]
    everyone = others(sizes)

    row_in = pltpu.make_async_copy(x_ref.at[pl.ds(rows - 1, 1)], rowbuf, in_sem.at[0])
    col_in = pltpu.make_async_copy(x_ref.at[:, pl.ds(cols - 2 * SUB, 2 * SUB), :], colbuf, in_sem.at[1])
    row_in.start()
    col_in.start()

    def chunk(k):
        return pltpu.make_async_copy(
            x_ref.at[pl.ds(k * BLOCK, BLOCK)], xv.at[pl.ds(k * BLOCK, BLOCK)], x_sem.at[k]
        )

    for k in range(steps):
        chunk(k).start()
    gate_in = [
        pltpu.make_async_copy(ref, gate.at[:, pl.ds(k * att, att)], in_sem.at[2 + k])
        for k, ref in enumerate((at_ref, as_ref))
    ]
    for copy in gate_in:
        copy.start()

    barrier = pltpu.get_barrier_semaphore()
    for device in everyone:
        pl.semaphore_signal(barrier, inc=1, device_id=device, device_id_type=MESH)

    wide = column(0.5 + 0.5 * delta_ref[...], mid)
    wrh[...] = (wr_ref[...].astype(F32) * wide).astype(BF16)
    wph[:mid, :] = (we_ref[...].astype(F32) * 0.5).astype(BF16)
    for k in range(cout // mid):
        at = slice(k * mid, (k + 1) * mid)
        wph[mid:, at] = (ws_ref[:, at].astype(F32) * wide).astype(BF16)
    none = jnp.zeros((mid, mid), BF16)
    for b in range(3):
        tap = [(sp_ref[a, b].astype(F32) * 0.5).astype(BF16) for a in range(3)]
        at = slice(b * mid, (b + 1) * mid)
        under = slice((3 + b) * mid, (4 + b) * mid)
        wf[at, :mid] = tap[1]
        wf[at, mid:] = none
        wf[under, :mid] = tap[2]
        wf[under, mid:] = tap[0]
        for k, a in enumerate((1, 2, 0)):
            if b == 0:
                wb[(2 * k + 1) * mid : (2 * k + 2) * mid, mid:] = tap[a]
                wb[2 * k * mid : (2 * k + 1) * mid, mid:] = none
            else:
                wb[(2 * k + b - 1) * mid : (2 * k + b) * mid, :mid] = tap[a]

    row_in.wait()
    col_in.wait()
    col = colbuf[:, SUB:, :].astype(F32)[:, SUB - 1, :].astype(BF16)
    edge, _ = silu_pair(dot(jnp.concatenate([rowbuf[0], col], axis=0), wrh[...]))
    edges1[...] = edge.astype(BF16)
    copies1 = edge_copies(
        edges1, landed1, es1, er1,
        ((0, cols, 0), (cols, rows, cols), (cols - 2 * SUB, 2 * SUB, cols + rows)),
        (shifted(sizes, 0, 1), shifted(sizes, 1, 0), shifted(sizes, 1, 1)),
    )

    def reduce_block(k):
        chunk(k).wait()
        for part in range(BLOCK // PART):
            at = pl.ds(k * BLOCK + part * PART, PART)
            act, slope = silu_pair(dot(xv[at].reshape(PART * cols, chan), wrh[...]))
            s1[at] = slope.reshape(PART, cols, mid).astype(s1.dtype)
            red[at, SUB:, :] = act.reshape(PART, cols, mid)

    reduce_block(0)
    pl.semaphore_wait(barrier, len(everyone))
    for copy in copies1:
        copy.start()
    for k in range(1, steps):
        reduce_block(k)
    for copy in gate_in:
        copy.wait()
    high, low = split(gate[...])
    ghigh[...] = high
    glow[...] = low
    for copy in copies1:
        copy.wait()
    above = jnp.where(lax.axis_index("space") > 0, 1.0, 0.0)
    beside = jnp.where(lax.axis_index("head") > 0, 1.0, 0.0)
    up[0:SUB, :] = landed1[cols + rows :, :].astype(F32)[SUB:] * (above * beside)
    up[SUB:, :] = landed1[0:cols, :].astype(F32) * above
    left[...] = landed1[cols : cols + rows, :].astype(F32) * beside
    for r in range(rows):
        red[r, SUB - 1 : SUB, :] = left[r : r + 1, :]
    sums[...] = jnp.zeros_like(sums)

    def taps_of(source):
        return [source[pl.ds(SUB - 1 + b, ocol, stride=2), :].astype(BF16) for b in range(3)]

    carry2[...] = dot(jnp.concatenate(taps_of(up), axis=1), wf[3 * mid :, mid:])

    def conv_block(k, none):
        trow = (k * ob) // half
        total = [jnp.zeros((SUB, cout), F32) for c in range(tiles_c)]
        above = carry2[...]
        for part in range(ob // LINES):
            first = pl.multiple_of(k * BLOCK, BLOCK) + 2 * part * LINES
            lines = [
                jnp.concatenate(taps_of(red.at[first + 2 * i]) + taps_of(red.at[first + 2 * i + 1]), axis=1)
                for i in range(LINES)
            ]
            y = dot(jnp.concatenate(lines, axis=0), wf[...])
            later = y[:, mid:]
            now = y[:, :mid] + jnp.concatenate([above, later[: (LINES - 1) * ocol]], axis=0)
            above = later[(LINES - 1) * ocol :]
            act, slope = silu_pair(now)
            slope = slope.reshape(LINES, ocol, mid)
            at = pl.ds(pl.multiple_of(k * ob, ob) + part * LINES, LINES)
            s2[at] = slope.astype(s2.dtype)
            col2[at, :] = slope[:, 0, :]
            short = []
            for i in range(LINES):
                slo[part * LINES + i] = xv[first + 2 * i, :, : chan // 2].astype(F32)
                shi[part * LINES + i] = xv[first + 2 * i, :, chan // 2 :].astype(F32)
                short.append(
                    jnp.concatenate(
                        [
                            room.at[part * LINES + i][pl.ds(0, ocol, stride=2), :].astype(BF16)
                            for room in (slo, shi)
                        ],
                        axis=1,
                    )
                )
            act, slope = silu_pair(
                dot(jnp.concatenate([act.astype(BF16), jnp.concatenate(short, axis=0)], axis=1), wph[...])
            )
            slope = slope.reshape(LINES, ocol, cout)
            s3[at] = slope.astype(s3.dtype)
            col3[at, :] = slope[:, 0, :]
            cells = jnp.sum(act.reshape(LINES, tiles_c, half // SUB, SUB, cout), axis=(0, 2))
            for c in range(tiles_c):
                total[c] = total[c] + cells[c]
        carry2[...] = above
        for c in range(tiles_c):
            slot = trow * tiles_c + c
            sums[slot] = sums[slot] + total[c]
        return none

    lax.fori_loop(0, steps, conv_block, 0)

    ao, cls = ao_ref[...], cls_ref[...]
    embed = jnp.sum(sums[...], axis=1) * (1.0 / (half * half))
    high, low = split(embed)
    first = dot(jnp.concatenate([high, low], axis=0), ghigh[...])
    gates = first[:slots] + first[slots:] + dot(high, glow[...])
    tval = jnp.tanh(gates[:, :att])
    gval = sigm(gates[:, att:])
    score = jnp.sum(tval * gval * ao, axis=1, keepdims=True)
    value = jnp.sum(embed * cls, axis=1, keepdims=True)
    slot = lax.broadcasted_iota(jnp.int32, (slots, 128), 0)
    marks = jnp.zeros(slot.shape, jnp.int32)
    for r in range(tiles_r):
        for c in range(tiles_c):
            mark = jnp.broadcast_to(tissue_ref[r : r + 1, c : c + 1], slot.shape)
            marks = jnp.where(slot == r * tiles_c + c, mark, marks)
    live = marks[:, 0:1] > 0
    top = jnp.max(jnp.where(live, score, -1e30), axis=0, keepdims=True)
    weight = jnp.where(live, jnp.exp(score - top), 0.0)
    lane = lax.broadcasted_iota(jnp.int32, (1, 128), 1)
    payload = jnp.where(
        lane == 0, top,
        jnp.where(
            lane == 1, jnp.sum(weight, axis=0, keepdims=True), jnp.sum(weight * value, axis=0, keepdims=True)
        ),
    )
    mine1[...] = payload
    got1[0] = payload
    for k, device in enumerate(everyone):
        remote(mine1, got1.at[k + 1], xs1.at[0], xr1.at[0], device).start()
    every1 = got1.at[pl.ds(1, len(everyone))]
    arrival1 = remote(every1, every1, xs1.at[0], xr1.at[0], everyone[0])
    dtanh = ao * gval * (1.0 - tval * tval)
    dsigm = ao * tval * gval * (1.0 - gval)
    high, low = split(jnp.concatenate([dtanh, dsigm], axis=1))
    first = dot_t(jnp.concatenate([high, low], axis=0), ghigh[...])
    slant = first[:slots] + first[slots:] + dot_t(high, glow[...])
    arrival1.wait()
    every = got1[...]
    best = jnp.max(every, axis=0)[:, 0:1]
    factor = jnp.exp(every[:, :, 0:1] - best[None])
    both = jnp.sum(every * factor, axis=0)
    total = both[:, 1:2]
    prob = jnp.where(live, jnp.exp(score - best), 0.0) / total
    gap = value - both[:, 2:3] / total
    dembed = prob * (cls + gap * slant) * (1.0 / (half * half))
    dembed_ref[...] = dembed

    def spread_rows(tiles):
        return jnp.concatenate([jnp.broadcast_to(dembed[t : t + 1], (half, cout)) for t in tiles], axis=0)

    line = jnp.concatenate([s3[0].astype(F32) * spread_rows(range(tiles_c)),
                            col3[...] * spread_rows(range(0, tiles_r * tiles_c, tiles_c))], axis=0).astype(BF16)
    line = dot_t(line, wph[:mid, :]) * jnp.concatenate([s2[0].astype(F32), col2[...]], axis=0)
    edges2[...] = line.astype(BF16)
    copies2 = edge_copies(
        edges2, landed2, es2, er2,
        ((0, ocol, 0), (ocol, orow, ocol), (0, 2 * SUB, ocol + orow)),
        (shifted(sizes, 0, -1), shifted(sizes, -1, 0), shifted(sizes, -1, -1)),
    )
    for copy in copies2:
        copy.start()

    def spatial_back(k, none):
        at = pl.ds(pl.multiple_of(k * ob, ob), ob)
        trow = (k * ob) // half
        spread = jnp.concatenate(
            [jnp.broadcast_to(dembed_ref[pl.ds(trow * tiles_c + c, 1), :], (half, cout)) for c in range(tiles_c)],
            axis=0,
        )
        dpre = (s3[at].astype(F32) * spread[None]).astype(BF16).reshape(ob * ocol, cout)
        both = dot_t(dpre, wph[...])
        dsx[at, 0:ocol, :] = both[:, :mid].reshape(ob, ocol, mid) * s2[at].astype(F32)
        for i in range(ob):
            line = both[i * ocol : (i + 1) * ocol]
            for c in range(2):
                room = red.at[pl.multiple_of(k * BLOCK, BLOCK) + 2 * i + c]
                room[pl.ds(0, ocol, stride=2), :] = line[:, mid + c * (chan // 2) : mid + (c + 1) * (chan // 2)]
                room[pl.ds(1, ocol, stride=2), :] = jnp.zeros((ocol, mid), F32)
        return none

    lax.fori_loop(0, steps, spatial_back, 0)
    for copy in copies2:
        copy.wait()
    below = jnp.where(lax.axis_index("space") < sizes[1] - 1, 1.0, 0.0)
    beside = jnp.where(lax.axis_index("head") < sizes[0] - 1, 1.0, 0.0)
    dsx[orow, 0:ocol, :] = landed2[0:ocol, :].astype(F32) * below
    dsx[orow, ocol:, :] = landed2[ocol + orow :, :].astype(F32)[:SUB] * (below * beside)
    left[0:orow, :] = landed2[ocol : ocol + orow, :].astype(F32) * beside
    for r in range(orow):
        dsx[r, ocol : ocol + 1, :] = left[r : r + 1, :]

    def pair(i):
        return jnp.concatenate([dsx[i, 0:ocol, :], dsx[i, 1 : ocol + 1, :]], axis=1).astype(BF16)

    carry3[...] = dot_t(pair(orow), wb[4 * mid :, :])
    total_ref[...] = jnp.zeros_like(total_ref)

    def reduced_back(step, none):
        k = steps - 1 - step
        first = pl.multiple_of(k * BLOCK, BLOCK)
        y = dot_t(jnp.concatenate([pair(k * ob + i) for i in range(ob)], axis=0), wb[...])
        for i in range(ob):
            at = slice(i * ocol, (i + 1) * ocol)
            below = carry3[...] if i == ob - 1 else y[(i + 1) * ocol : (i + 2) * ocol, 4 * mid :]
            odd = y[at, 2 * mid : 4 * mid] + below
            for dj in range(2):
                side = slice(dj * mid, (dj + 1) * mid)
                drs[2 * i, pl.ds(dj, ocol, stride=2), :] = y[at, side]
                drs[2 * i + 1, pl.ds(dj, ocol, stride=2), :] = odd[:, side]
        carry3[...] = y[0:ocol, 4 * mid :]
        dred = (drs[...] * s1[pl.ds(first, BLOCK)].astype(F32)).astype(BF16)
        dinput = dot_t(dred.reshape(BLOCK * cols, mid), wrh[...]).reshape(BLOCK, cols, chan)
        total = jnp.zeros((SUB, chan), F32)
        for r in range(BLOCK):
            value = dinput[r]
            if r % 2 == 0:
                value = value + jnp.concatenate([red[first + r, 0:cols, :], red[first + r + 1, 0:cols, :]], axis=1)
            out_ref[first + r] = value.astype(BF16)
            total = total + jnp.sum((value * xv[first + r].astype(F32)).reshape(cols // SUB, SUB, chan), axis=0)
        total_ref[...] += total
        return none

    lax.fori_loop(0, steps, reduced_back, 0)

    part = jnp.sum(total_ref[...], axis=0, keepdims=True)
    lines = chan // 128
    part = jnp.concatenate([part[:, k * 128 : (k + 1) * 128] for k in range(lines)], axis=0)
    mine2[...] = part
    got2[0] = part
    for k, device in enumerate(everyone):
        remote(mine2, got2.at[k + 1], xs2.at[0], xr2.at[0], device).start()
    every2 = got2.at[pl.ds(1, len(everyone))]
    arrival2 = remote(every2, every2, xs2.at[0], xr2.at[0], everyone[0])
    arrival2.wait()
    part = jnp.sum(got2[...], axis=0)
    delta = delta_ref[...]
    ddelta = jnp.concatenate([part[k : k + 1] for k in range(lines)], axis=1) / (1.0 + delta)
    norm = jnp.sqrt(jnp.sum(ddelta * ddelta, axis=1, keepdims=True) * (1.0 / chan) + 1e-06)
    result = delta + (2 * dir_ref[...] - 1).astype(F32) * float(ALPHA) * ddelta / norm
    delta_out[...] = result.reshape(chan)


def leave_kernel(v_ref, out_ref, sem):
    n = sem.shape[0]
    size = v_ref.shape[0] // n
    copies = [
        pltpu.make_async_copy(v_ref.at[pl.ds(k * size, size)], out_ref.at[pl.ds(k * size, size)], sem.at[k])
        for k in range(n)
    ]
    for copy in copies:
        copy.start()
    for copy in copies:
        copy.wait()


def shards(
    features, stain_delta, tissue, reduce_weight, spatial_weight, expand_weight, shortcut_weight, attn_tanh, attn_sigm,
    attn_out, classifier, step_dir,
):
    rows, cols, chan = features.shape
    mid = reduce_weight.shape[1]
    cout = expand_weight.shape[1]
    att = attn_out.shape[0]
    tiles_r, tiles_c = tissue.shape
    slots = -(-tiles_r * tiles_c // SUB) * SUB
    orow, ocol = rows // 2, cols // 2
    sizes = tuple(lax.axis_size(axis) for axis in AXES)
    n = sizes[0] * sizes[1]
    steps = rows // BLOCK
    ob = BLOCK // 2
    vmem = pl.BlockSpec(memory_space=pltpu.VMEM)
    hbm = pl.BlockSpec(memory_space=pl.ANY)
    V, D = pltpu.VMEM, pltpu.SemaphoreType.DMA

    grad, new_delta = pl.pallas_call(
        functools.partial(whole_kernel, sizes),
        out_shape=(OUT_SPACE((rows, cols, chan), BF16), jax.ShapeDtypeStruct((chan,), F32)),
        in_specs=[hbm, vmem, vmem, vmem, vmem, vmem, vmem, vmem, hbm, hbm, vmem, vmem],
        out_specs=(vmem, vmem),
        scratch_shapes=[
            V((rows, cols, chan), BF16),
            V((rows, cols + SUB, mid), F32),
            V((rows, cols, mid), F32),
            V((orow, ocol, mid), F32),
            V((orow, ocol, cout), F32),
            V((orow + 1, ocol + SUB, mid), F32),
            V((BLOCK, cols, mid), F32),
            V((ob, cols, chan // 2), F32),
            V((ob, cols, chan // 2), F32),
            V((chan, mid), BF16),
            V((mid + chan, cout), BF16),
            V((6 * mid, 2 * mid), BF16),
            V((6 * mid, 2 * mid), BF16),
            V((cout, 2 * att), F32),
            V((cout, 2 * att), BF16),
            V((cout, 2 * att), BF16),
            V((slots, SUB, cout), F32),
            V((orow, mid), F32),
            V((orow, cout), F32),
            V((ocol, mid), F32),
            V((ocol, 2 * mid), F32),
            V((1, cols, chan), BF16),
            V((rows, 2 * SUB, chan), BF16),
            V((cols + SUB, mid), F32),
            V((rows, mid), F32),
            V((cols + rows, mid), BF16),
            V((cols + rows + 2 * SUB, mid), BF16),
            V((ocol + orow, mid), BF16),
            V((ocol + orow + 2 * SUB, mid), BF16),
            V((1, 128), F32),
            V((n, 1, 128), F32),
            V((chan // 128, 128), F32),
            V((n, chan // 128, 128), F32),
            V((slots, cout), F32),
            V((SUB, chan), F32),
            D((steps,)),
            D((4,)),
            D((3,)),
            D((3,)),
            D((3,)),
            D((3,)),
            D((1,)),
            D((1,)),
            D((1,)),
            D((1,)),
        ],
        compiler_params=pltpu.CompilerParams(
            vmem_limit_bytes=52 * 1024 * 1024, collective_id=0, has_side_effects=True
        ),
        name="slide",
    )(
        features, stain_delta[None, :], step_dir[None, :], tissue, reduce_weight, spatial_weight, expand_weight,
        shortcut_weight, attn_tanh, attn_sigm, attn_out[None, :], classifier[None, :],
    )
    feature_grad = pl.pallas_call(
        leave_kernel,
        out_shape=jax.ShapeDtypeStruct((rows, cols, chan), BF16),
        in_specs=[vmem],
        out_specs=hbm,
        scratch_shapes=[D((4,))],
        compiler_params=pltpu.CompilerParams(vmem_limit_bytes=1024 * 1024),
        name="leave",
    )(grad)
    return (feature_grad, new_delta)


def OUT_SPACE(shape, dtype):
    return pltpu.VMEM(shape, dtype)


def solution(mesh):
    return jax.shard_map(
        shards,
        mesh=mesh,
        in_specs=(P("space", "head", None), P(), P("space", "head")) + (P(),) * 9,
        out_specs=(P("space", "head", None), P()),
        check_vma=False,
    )
```

```python
import functools

import jax
import jax.numpy as jnp
from jax import lax
from jax.experimental import pallas as pl
from jax.experimental.pallas import tpu as pltpu
from jax.sharding import PartitionSpec as P

TILE = 64
ALPHA = 1
BLOCK = 32
SUB = 8
PART = 8
LINES = 8
F32 = jnp.float32
BF16 = jnp.bfloat16
MESH = pl.DeviceIdType.MESH
AXES = ("head", "space")


def sigm(value):
    return 0.5 + 0.5 * jnp.tanh(0.5 * value)


def silu_pair(h):
    t = jnp.tanh(h)
    u = 1.0 + t
    act = h * u
    return act, u + act * (1.0 - t)


def dot(a, b):
    return jnp.dot(a, b, preferred_element_type=F32)


def dot_t(a, b):
    return lax.dot_general(a, b, (((1,), (1,)), ((), ())), preferred_element_type=F32)


def column(row, width):
    return jnp.transpose(jnp.broadcast_to(row, (width, row.shape[1])))


def split(value):
    high = value.astype(BF16)
    return high, (value - high.astype(F32)).astype(BF16)


def shifted(sizes, a, b):
    return (
        lax.rem(lax.axis_index(AXES[0]) + sizes[0] + a, sizes[0]),
        lax.rem(lax.axis_index(AXES[1]) + sizes[1] + b, sizes[1]),
    )


def others(sizes):
    return [shifted(sizes, a, b) for a in range(sizes[0]) for b in range(sizes[1]) if a + b > 0]


def remote(source, target, send, recv, device):
    return pltpu.make_async_remote_copy(
        src_ref=source, dst_ref=target, send_sem=send, recv_sem=recv, device_id=device, device_id_type=MESH
    )


def edge_copies(edges, landed, send, recv, spans, targets):
    return [
        remote(edges.at[pl.ds(source, size)], landed.at[pl.ds(place, size)], send.at[k], recv.at[k], targets[k])
        for k, (source, size, place) in enumerate(spans)
    ]


def whole_kernel(
    sizes, x_ref, delta_ref, dir_ref, tissue_ref, wr_ref, sp_ref, we_ref, ws_ref, at_ref, as_ref, ao_ref, cls_ref,
    out_ref, delta_out,
    xv, red, s1, s2, s3, dsx, drs, slo, shi, wrh, wph, wf, wb, gate, ghigh, glow, sums, col2, col3, carry2, carry3,
    rowbuf, colbuf, up, left, edges1, landed1, edges2, landed2, mine1, got1, mine2, got2, dembed_ref, total_ref,
    x_sem, in_sem, es1, er1, es2, er2, xs1, xr1, xs2, xr2,
):
    rows, cols, chan = xv.shape
    mid, cout = we_ref.shape
    orow, ocol = rows // 2, cols // 2
    half = TILE // 2
    tiles_r, tiles_c = tissue_ref.shape
    slots = sums.shape[0]
    steps = rows // BLOCK
    ob = BLOCK // 2
    att = ao_ref.shape[1]
    everyone = others(sizes)

    row_in = pltpu.make_async_copy(x_ref.at[pl.ds(rows - 1, 1)], rowbuf, in_sem.at[0])
    col_in = pltpu.make_async_copy(x_ref.at[:, pl.ds(cols - 2 * SUB, 2 * SUB), :], colbuf, in_sem.at[1])
    row_in.start()
    col_in.start()

    def chunk(k):
        return pltpu.make_async_copy(
            x_ref.at[pl.ds(k * BLOCK, BLOCK)], xv.at[pl.ds(k * BLOCK, BLOCK)], x_sem.at[k]
        )

    for k in range(steps):
        chunk(k).start()
    gate_in = [
        pltpu.make_async_copy(ref, gate.at[:, pl.ds(k * att, att)], in_sem.at[2 + k])
        for k, ref in enumerate((at_ref, as_ref))
    ]
    for copy in gate_in:
        copy.start()

    barrier = pltpu.get_barrier_semaphore()
    for device in everyone:
        pl.semaphore_signal(barrier, inc=1, device_id=device, device_id_type=MESH)

    wide = column(0.5 + 0.5 * delta_ref[...], mid)
    wrh[...] = (wr_ref[...].astype(F32) * wide).astype(BF16)
    wph[:mid, :] = (we_ref[...].astype(F32) * 0.5).astype(BF16)
    for k in range(cout // mid):
        at = slice(k * mid, (k + 1) * mid)
        wph[mid:, at] = (ws_ref[:, at].astype(F32) * wide).astype(BF16)
    none = jnp.zeros((mid, mid), BF16)
    for b in range(3):
        tap = [(sp_ref[a, b].astype(F32) * 0.5).astype(BF16) for a in range(3)]
        at = slice(b * mid, (b + 1) * mid)
        under = slice((3 + b) * mid, (4 + b) * mid)
        wf[at, :mid] = tap[1]
        wf[at, mid:] = none
        wf[under, :mid] = tap[2]
        wf[under, mid:] = tap[0]
        for k, a in enumerate((1, 2, 0)):
            if b == 0:
                wb[(2 * k + 1) * mid : (2 * k + 2) * mid, mid:] = tap[a]
                wb[2 * k * mid : (2 * k + 1) * mid, mid:] = none
            else:
                wb[(2 * k + b - 1) * mid : (2 * k + b) * mid, :mid] = tap[a]

    def reduce_block(k):
        chunk(k).wait()
        for part in range(BLOCK // PART):
            at = pl.ds(k * BLOCK + part * PART, PART)
            act, slope = silu_pair(dot(xv[at].reshape(PART * cols, chan), wrh[...]))
            s1[at] = slope.reshape(PART, cols, mid).astype(s1.dtype)
            red[at, SUB:, :] = act.reshape(PART, cols, mid)

    reduce_block(0)
    row_in.wait()
    col_in.wait()
    col = colbuf[:, SUB:, :].astype(F32)[:, SUB - 1, :].astype(BF16)
    edge, _ = silu_pair(dot(jnp.concatenate([rowbuf[0], col], axis=0), wrh[...]))
    edges1[...] = edge.astype(BF16)
    copies1 = edge_copies(
        edges1, landed1, es1, er1,
        ((0, cols, 0), (cols, rows, cols), (cols - 2 * SUB, 2 * SUB, cols + rows)),
        (shifted(sizes, 0, 1), shifted(sizes, 1, 0), shifted(sizes, 1, 1)),
    )
    pl.semaphore_wait(barrier, len(everyone))
    for copy in copies1:
        copy.start()
    for k in range(1, steps):
        reduce_block(k)
    for copy in gate_in:
        copy.wait()
    high, low = split(gate[...])
    ghigh[...] = high
    glow[...] = low
    for copy in copies1:
        copy.wait()
    above = jnp.where(lax.axis_index("space") > 0, 1.0, 0.0)
    beside = jnp.where(lax.axis_index("head") > 0, 1.0, 0.0)
    up[0:SUB, :] = landed1[cols + rows :, :].astype(F32)[SUB:] * (above * beside)
    up[SUB:, :] = landed1[0:cols, :].astype(F32) * above
    left[...] = landed1[cols : cols + rows, :].astype(F32) * beside
    for r in range(rows):
        red[r, SUB - 1 : SUB, :] = left[r : r + 1, :]
    sums[...] = jnp.zeros_like(sums)

    def taps_of(source):
        return [source[pl.ds(SUB - 1 + b, ocol, stride=2), :].astype(BF16) for b in range(3)]

    carry2[...] = dot(jnp.concatenate(taps_of(up), axis=1), wf[3 * mid :, mid:])

    def conv_block(k, none):
        trow = (k * ob) // half
        total = [jnp.zeros((SUB, cout), F32) for c in range(tiles_c)]
        above = carry2[...]
        for part in range(ob // LINES):
            first = pl.multiple_of(k * BLOCK, BLOCK) + 2 * part * LINES
            lines = [
                jnp.concatenate(taps_of(red.at[first + 2 * i]) + taps_of(red.at[first + 2 * i + 1]), axis=1)
                for i in range(LINES)
            ]
            y = dot(jnp.concatenate(lines, axis=0), wf[...])
            later = y[:, mid:]
            now = y[:, :mid] + jnp.concatenate([above, later[: (LINES - 1) * ocol]], axis=0)
            above = later[(LINES - 1) * ocol :]
            act, slope = silu_pair(now)
            slope = slope.reshape(LINES, ocol, mid)
            at = pl.ds(pl.multiple_of(k * ob, ob) + part * LINES, LINES)
            s2[at] = slope.astype(s2.dtype)
            col2[at, :] = slope[:, 0, :]
            short = []
            for i in range(LINES):
                slo[part * LINES + i] = xv[first + 2 * i, :, : chan // 2].astype(F32)
                shi[part * LINES + i] = xv[first + 2 * i, :, chan // 2 :].astype(F32)
                short.append(
                    jnp.concatenate(
                        [
                            room.at[part * LINES + i][pl.ds(0, ocol, stride=2), :].astype(BF16)
                            for room in (slo, shi)
                        ],
                        axis=1,
                    )
                )
            act, slope = silu_pair(
                dot(jnp.concatenate([act.astype(BF16), jnp.concatenate(short, axis=0)], axis=1), wph[...])
            )
            slope = slope.reshape(LINES, ocol, cout)
            s3[at] = slope.astype(s3.dtype)
            col3[at, :] = slope[:, 0, :]
            cells = jnp.sum(act.reshape(LINES, tiles_c, half // SUB, SUB, cout), axis=(0, 2))
            for c in range(tiles_c):
                total[c] = total[c] + cells[c]
        carry2[...] = above
        for c in range(tiles_c):
            slot = trow * tiles_c + c
            sums[slot] = sums[slot] + total[c]
        return none

    lax.fori_loop(0, steps, conv_block, 0)

    ao, cls = ao_ref[...], cls_ref[...]
    embed = jnp.sum(sums[...], axis=1) * (1.0 / (half * half))
    high, low = split(embed)
    first = dot(jnp.concatenate([high, low], axis=0), ghigh[...])
    gates = first[:slots] + first[slots:] + dot(high, glow[...])
    tval = jnp.tanh(gates[:, :att])
    gval = sigm(gates[:, att:])
    score = jnp.sum(tval * gval * ao, axis=1, keepdims=True)
    value = jnp.sum(embed * cls, axis=1, keepdims=True)
    slot = lax.broadcasted_iota(jnp.int32, (slots, 128), 0)
    marks = jnp.zeros(slot.shape, jnp.int32)
    for r in range(tiles_r):
        for c in range(tiles_c):
            mark = jnp.broadcast_to(tissue_ref[r : r + 1, c : c + 1], slot.shape)
            marks = jnp.where(slot == r * tiles_c + c, mark, marks)
    live = marks[:, 0:1] > 0
    top = jnp.max(jnp.where(live, score, -1e30), axis=0, keepdims=True)
    weight = jnp.where(live, jnp.exp(score - top), 0.0)
    lane = lax.broadcasted_iota(jnp.int32, (1, 128), 1)
    payload = jnp.where(
        lane == 0, top,
        jnp.where(
            lane == 1, jnp.sum(weight, axis=0, keepdims=True), jnp.sum(weight * value, axis=0, keepdims=True)
        ),
    )
    mine1[...] = payload
    got1[0] = payload
    for k, device in enumerate(everyone):
        remote(mine1, got1.at[k + 1], xs1.at[0], xr1.at[0], device).start()
    every1 = got1.at[pl.ds(1, len(everyone))]
    arrival1 = remote(every1, every1, xs1.at[0], xr1.at[0], everyone[0])
    dtanh = ao * gval * (1.0 - tval * tval)
    dsigm = ao * tval * gval * (1.0 - gval)
    high, low = split(jnp.concatenate([dtanh, dsigm], axis=1))
    first = dot_t(jnp.concatenate([high, low], axis=0), ghigh[...])
    slant = first[:slots] + first[slots:] + dot_t(high, glow[...])
    arrival1.wait()
    every = got1[...]
    best = jnp.max(every, axis=0)[:, 0:1]
    factor = jnp.exp(every[:, :, 0:1] - best[None])
    both = jnp.sum(every * factor, axis=0)
    total = both[:, 1:2]
    prob = jnp.where(live, jnp.exp(score - best), 0.0) / total
    gap = value - both[:, 2:3] / total
    dembed = prob * (cls + gap * slant) * (1.0 / (half * half))
    dembed_ref[...] = dembed

    def spread_rows(tiles):
        return jnp.concatenate([jnp.broadcast_to(dembed[t : t + 1], (half, cout)) for t in tiles], axis=0)

    line = jnp.concatenate([s3[0].astype(F32) * spread_rows(range(tiles_c)),
                            col3[...] * spread_rows(range(0, tiles_r * tiles_c, tiles_c))], axis=0).astype(BF16)
    line = dot_t(line, wph[:mid, :]) * jnp.concatenate([s2[0].astype(F32), col2[...]], axis=0)
    edges2[...] = line.astype(BF16)
    copies2 = edge_copies(
        edges2, landed2, es2, er2,
        ((0, ocol, 0), (ocol, orow, ocol), (0, 2 * SUB, ocol + orow)),
        (shifted(sizes, 0, -1), shifted(sizes, -1, 0), shifted(sizes, -1, -1)),
    )
    for copy in copies2:
        copy.start()

    def spatial_back(k, none):
        at = pl.ds(pl.multiple_of(k * ob, ob), ob)
        trow = (k * ob) // half
        spread = jnp.concatenate(
            [jnp.broadcast_to(dembed_ref[pl.ds(trow * tiles_c + c, 1), :], (half, cout)) for c in range(tiles_c)],
            axis=0,
        )
        dpre = (s3[at].astype(F32) * spread[None]).astype(BF16).reshape(ob * ocol, cout)
        both = dot_t(dpre, wph[...])
        dsx[at, 0:ocol, :] = both[:, :mid].reshape(ob, ocol, mid) * s2[at].astype(F32)
        for i in range(ob):
            line = both[i * ocol : (i + 1) * ocol]
            for c in range(2):
                room = red.at[pl.multiple_of(k * BLOCK, BLOCK) + 2 * i + c]
                room[pl.ds(0, ocol, stride=2), :] = line[:, mid + c * (chan // 2) : mid + (c + 1) * (chan // 2)]
                room[pl.ds(1, ocol, stride=2), :] = jnp.zeros((ocol, mid), F32)
        return none

    lax.fori_loop(0, steps, spatial_back, 0, unroll=True)
    for copy in copies2:
        copy.wait()
    below = jnp.where(lax.axis_index("space") < sizes[1] - 1, 1.0, 0.0)
    beside = jnp.where(lax.axis_index("head") < sizes[0] - 1, 1.0, 0.0)
    dsx[orow, 0:ocol, :] = landed2[0:ocol, :].astype(F32) * below
    dsx[orow, ocol:, :] = landed2[ocol + orow :, :].astype(F32)[:SUB] * (below * beside)
    left[0:orow, :] = landed2[ocol : ocol + orow, :].astype(F32) * beside
    for r in range(orow):
        dsx[r, ocol : ocol + 1, :] = left[r : r + 1, :]

    def pair(i):
        return jnp.concatenate([dsx[i, 0:ocol, :], dsx[i, 1 : ocol + 1, :]], axis=1).astype(BF16)

    carry3[...] = dot_t(pair(orow), wb[4 * mid :, :])
    total_ref[...] = jnp.zeros_like(total_ref)

    def reduced_back(step, none):
        k = steps - 1 - step
        first = pl.multiple_of(k * BLOCK, BLOCK)
        y = dot_t(jnp.concatenate([pair(k * ob + i) for i in range(ob)], axis=0), wb[...])
        for i in range(ob):
            at = slice(i * ocol, (i + 1) * ocol)
            below = carry3[...] if i == ob - 1 else y[(i + 1) * ocol : (i + 2) * ocol, 4 * mid :]
            odd = y[at, 2 * mid : 4 * mid] + below
            for dj in range(2):
                side = slice(dj * mid, (dj + 1) * mid)
                drs[2 * i, pl.ds(dj, ocol, stride=2), :] = y[at, side]
                drs[2 * i + 1, pl.ds(dj, ocol, stride=2), :] = odd[:, side]
        carry3[...] = y[0:ocol, 4 * mid :]
        dred = (drs[...] * s1[pl.ds(first, BLOCK)].astype(F32)).astype(BF16)
        dinput = dot_t(dred.reshape(BLOCK * cols, mid), wrh[...]).reshape(BLOCK, cols, chan)
        total = jnp.zeros((SUB, chan), F32)
        for r in range(BLOCK):
            value = dinput[r]
            if r % 2 == 0:
                value = value + jnp.concatenate([red[first + r, 0:cols, :], red[first + r + 1, 0:cols, :]], axis=1)
            out_ref[first + r] = value.astype(BF16)
            total = total + jnp.sum((value * xv[first + r].astype(F32)).reshape(cols // SUB, SUB, chan), axis=0)
        total_ref[...] += total
        return none

    lax.fori_loop(0, steps, reduced_back, 0, unroll=True)

    part = jnp.sum(total_ref[...], axis=0, keepdims=True)
    lines = chan // 128
    part = jnp.concatenate([part[:, k * 128 : (k + 1) * 128] for k in range(lines)], axis=0)
    mine2[...] = part
    got2[0] = part
    for k, device in enumerate(everyone):
        remote(mine2, got2.at[k + 1], xs2.at[0], xr2.at[0], device).start()
    every2 = got2.at[pl.ds(1, len(everyone))]
    arrival2 = remote(every2, every2, xs2.at[0], xr2.at[0], everyone[0])
    arrival2.wait()
    part = jnp.sum(got2[...], axis=0)
    delta = delta_ref[...]
    ddelta = jnp.concatenate([part[k : k + 1] for k in range(lines)], axis=1) / (1.0 + delta)
    norm = jnp.sqrt(jnp.sum(ddelta * ddelta, axis=1, keepdims=True) * (1.0 / chan) + 1e-06)
    result = delta + (2 * dir_ref[...] - 1).astype(F32) * float(ALPHA) * ddelta / norm
    delta_out[...] = result.reshape(chan)


def leave_kernel(v_ref, out_ref, sem):
    n = sem.shape[0]
    size = v_ref.shape[0] // n
    copies = [
        pltpu.make_async_copy(v_ref.at[pl.ds(k * size, size)], out_ref.at[pl.ds(k * size, size)], sem.at[k])
        for k in range(n)
    ]
    for copy in copies:
        copy.start()
    for copy in copies:
        copy.wait()


def shards(
    features, stain_delta, tissue, reduce_weight, spatial_weight, expand_weight, shortcut_weight, attn_tanh, attn_sigm,
    attn_out, classifier, step_dir,
):
    rows, cols, chan = features.shape
    mid = reduce_weight.shape[1]
    cout = expand_weight.shape[1]
    att = attn_out.shape[0]
    tiles_r, tiles_c = tissue.shape
    slots = -(-tiles_r * tiles_c // SUB) * SUB
    orow, ocol = rows // 2, cols // 2
    sizes = tuple(lax.axis_size(axis) for axis in AXES)
    n = sizes[0] * sizes[1]
    steps = rows // BLOCK
    ob = BLOCK // 2
    vmem = pl.BlockSpec(memory_space=pltpu.VMEM)
    hbm = pl.BlockSpec(memory_space=pl.ANY)
    V, D = pltpu.VMEM, pltpu.SemaphoreType.DMA

    grad, new_delta = pl.pallas_call(
        functools.partial(whole_kernel, sizes),
        out_shape=(OUT_SPACE((rows, cols, chan), BF16), jax.ShapeDtypeStruct((chan,), F32)),
        in_specs=[hbm, vmem, vmem, vmem, vmem, vmem, vmem, vmem, hbm, hbm, vmem, vmem],
        out_specs=(vmem, vmem),
        scratch_shapes=[
            V((rows, cols, chan), BF16),
            V((rows, cols + SUB, mid), F32),
            V((rows, cols, mid), F32),
            V((orow, ocol, mid), F32),
            V((orow, ocol, cout), F32),
            V((orow + 1, ocol + SUB, mid), F32),
            V((BLOCK, cols, mid), F32),
            V((ob, cols, chan // 2), F32),
            V((ob, cols, chan // 2), F32),
            V((chan, mid), BF16),
            V((mid + chan, cout), BF16),
            V((6 * mid, 2 * mid), BF16),
            V((6 * mid, 2 * mid), BF16),
            V((cout, 2 * att), F32),
            V((cout, 2 * att), BF16),
            V((cout, 2 * att), BF16),
            V((slots, SUB, cout), F32),
            V((orow, mid), F32),
            V((orow, cout), F32),
            V((ocol, mid), F32),
            V((ocol, 2 * mid), F32),
            V((1, cols, chan), BF16),
            V((rows, 2 * SUB, chan), BF16),
            V((cols + SUB, mid), F32),
            V((rows, mid), F32),
            V((cols + rows, mid), BF16),
            V((cols + rows + 2 * SUB, mid), BF16),
            V((ocol + orow, mid), BF16),
            V((ocol + orow + 2 * SUB, mid), BF16),
            V((1, 128), F32),
            V((n, 1, 128), F32),
            V((chan // 128, 128), F32),
            V((n, chan // 128, 128), F32),
            V((slots, cout), F32),
            V((SUB, chan), F32),
            D((steps,)),
            D((4,)),
            D((3,)),
            D((3,)),
            D((3,)),
            D((3,)),
            D((1,)),
            D((1,)),
            D((1,)),
            D((1,)),
        ],
        compiler_params=pltpu.CompilerParams(
            vmem_limit_bytes=52 * 1024 * 1024, collective_id=0, has_side_effects=True
        ),
        name="slide",
    )(
        features, stain_delta[None, :], step_dir[None, :], tissue, reduce_weight, spatial_weight, expand_weight,
        shortcut_weight, attn_tanh, attn_sigm, attn_out[None, :], classifier[None, :],
    )
    feature_grad = pl.pallas_call(
        leave_kernel,
        out_shape=jax.ShapeDtypeStruct((rows, cols, chan), BF16),
        in_specs=[vmem],
        out_specs=hbm,
        scratch_shapes=[D((4,))],
        compiler_params=pltpu.CompilerParams(vmem_limit_bytes=1024 * 1024),
        name="leave",
    )(grad)
    return (feature_grad, new_delta)


def OUT_SPACE(shape, dtype):
    return pltpu.VMEM(shape, dtype)


def solution(mesh):
    return jax.shard_map(
        shards,
        mesh=mesh,
        in_specs=(P("space", "head", None), P(), P("space", "head")) + (P(),) * 9,
        out_specs=(P("space", "head", None), P()),
        check_vma=False,
    )
```

```python
import functools

import jax
import jax.numpy as jnp
from jax import lax
from jax.experimental import pallas as pl
from jax.experimental.pallas import tpu as pltpu
from jax.sharding import PartitionSpec as P

TILE = 64
ALPHA = 1
BLOCK = 32
SUB = 8
PART = 8
LINES = 8
F32 = jnp.float32
BF16 = jnp.bfloat16
MESH = pl.DeviceIdType.MESH
AXES = ("head", "space")


def sigm(value):
    return 0.5 + 0.5 * jnp.tanh(0.5 * value)


def silu_pair(h):
    t = jnp.tanh(h)
    u = 1.0 + t
    act = h * u
    return act, u + act * (1.0 - t)


def dot(a, b):
    return jnp.dot(a, b, preferred_element_type=F32)


def dot_t(a, b):
    return lax.dot_general(a, b, (((1,), (1,)), ((), ())), preferred_element_type=F32)


def column(row, width):
    return jnp.transpose(jnp.broadcast_to(row, (width, row.shape[1])))


def split(value):
    high = value.astype(BF16)
    return high, (value - high.astype(F32)).astype(BF16)


def shifted(sizes, a, b):
    return (
        lax.rem(lax.axis_index(AXES[0]) + sizes[0] + a, sizes[0]),
        lax.rem(lax.axis_index(AXES[1]) + sizes[1] + b, sizes[1]),
    )


def others(sizes):
    return [shifted(sizes, a, b) for a in range(sizes[0]) for b in range(sizes[1]) if a + b > 0]


def remote(source, target, send, recv, device):
    return pltpu.make_async_remote_copy(
        src_ref=source, dst_ref=target, send_sem=send, recv_sem=recv, device_id=device, device_id_type=MESH
    )


def edge_copies(edges, landed, send, recv, spans, targets):
    return [
        remote(edges.at[pl.ds(source, size)], landed.at[pl.ds(place, size)], send.at[k], recv.at[k], targets[k])
        for k, (source, size, place) in enumerate(spans)
    ]


def whole_kernel(
    sizes, x_ref, delta_ref, dir_ref, tissue_ref, wr_ref, sp_ref, we_ref, ws_ref, at_ref, as_ref, ao_ref, cls_ref,
    out_ref, delta_out,
    xv, red, s1, s2, s3, dsx, drs, slo, shi, wrh, wph, wf, wb, gate, ghigh, glow, sums, col2, col3, carry2, carry3,
    rowbuf, colbuf, up, left, edges1, landed1, edges2, landed2, mine1, got1, mine2, got2, dembed_ref, total_ref,
    x_sem, in_sem, es1, er1, es2, er2, xs1, xr1, xs2, xr2,
):
    rows, cols, chan = xv.shape
    mid, cout = we_ref.shape
    orow, ocol = rows // 2, cols // 2
    half = TILE // 2
    tiles_r, tiles_c = tissue_ref.shape
    slots = sums.shape[0]
    steps = rows // BLOCK
    ob = BLOCK // 2
    piece = BLOCK // 2
    att = ao_ref.shape[1]
    everyone = others(sizes)

    row_in = pltpu.make_async_copy(x_ref.at[pl.ds(rows - 1, 1)], rowbuf, in_sem.at[0])
    col_in = pltpu.make_async_copy(x_ref.at[:, pl.ds(cols - 2 * SUB, 2 * SUB), :], colbuf, in_sem.at[1])
    row_in.start()
    col_in.start()

    def chunk(k):
        return pltpu.make_async_copy(
            x_ref.at[pl.ds(k * BLOCK, BLOCK)], xv.at[pl.ds(k * BLOCK, BLOCK)], x_sem.at[k]
        )

    for k in range(steps):
        chunk(k).start()
    gate_in = [
        pltpu.make_async_copy(ref, gate.at[:, pl.ds(k * att, att)], in_sem.at[2 + k])
        for k, ref in enumerate((at_ref, as_ref))
    ]
    for copy in gate_in:
        copy.start()

    barrier = pltpu.get_barrier_semaphore()
    for device in everyone:
        pl.semaphore_signal(barrier, inc=1, device_id=device, device_id_type=MESH)

    wide = column(0.5 + 0.5 * delta_ref[...], mid)
    wrh[...] = (wr_ref[...].astype(F32) * wide).astype(BF16)
    wph[:mid, :] = (we_ref[...].astype(F32) * 0.5).astype(BF16)
    for k in range(cout // mid):
        at = slice(k * mid, (k + 1) * mid)
        wph[mid:, at] = (ws_ref[:, at].astype(F32) * wide).astype(BF16)
    none = jnp.zeros((mid, mid), BF16)
    for b in range(3):
        tap = [(sp_ref[a, b].astype(F32) * 0.5).astype(BF16) for a in range(3)]
        at = slice(b * mid, (b + 1) * mid)
        under = slice((3 + b) * mid, (4 + b) * mid)
        wf[at, :mid] = tap[1]
        wf[at, mid:] = none
        wf[under, :mid] = tap[2]
        wf[under, mid:] = tap[0]
        for k, a in enumerate((1, 2, 0)):
            if b == 0:
                wb[(2 * k + 1) * mid : (2 * k + 2) * mid, mid:] = tap[a]
                wb[2 * k * mid : (2 * k + 1) * mid, mid:] = none
            else:
                wb[(2 * k + b - 1) * mid : (2 * k + b) * mid, :mid] = tap[a]

    def reduce_block(k):
        chunk(k).wait()
        for part in range(BLOCK // PART):
            at = pl.ds(k * BLOCK + part * PART, PART)
            act, slope = silu_pair(dot(xv[at].reshape(PART * cols, chan), wrh[...]))
            s1[at] = slope.reshape(PART, cols, mid).astype(s1.dtype)
            red[at, SUB:, :] = act.reshape(PART, cols, mid)

    reduce_block(0)
    row_in.wait()
    col_in.wait()
    col = colbuf[:, SUB:, :].astype(F32)[:, SUB - 1, :].astype(BF16)
    edge, _ = silu_pair(dot(jnp.concatenate([rowbuf[0], col], axis=0), wrh[...]))
    edges1[...] = edge.astype(BF16)
    copies1 = edge_copies(
        edges1, landed1, es1, er1,
        ((0, cols, 0), (cols, rows, cols), (cols - 2 * SUB, 2 * SUB, cols + rows)),
        (shifted(sizes, 0, 1), shifted(sizes, 1, 0), shifted(sizes, 1, 1)),
    )
    pl.semaphore_wait(barrier, len(everyone))
    for copy in copies1:
        copy.start()
    for k in range(1, steps):
        reduce_block(k)
    for copy in gate_in:
        copy.wait()
    high, low = split(gate[...])
    ghigh[...] = high
    glow[...] = low
    for copy in copies1:
        copy.wait()
    above = jnp.where(lax.axis_index("space") > 0, 1.0, 0.0)
    beside = jnp.where(lax.axis_index("head") > 0, 1.0, 0.0)
    up[0:SUB, :] = landed1[cols + rows :, :].astype(F32)[SUB:] * (above * beside)
    up[SUB:, :] = landed1[0:cols, :].astype(F32) * above
    left[...] = landed1[cols : cols + rows, :].astype(F32) * beside
    for r in range(rows):
        red[r, SUB - 1 : SUB, :] = left[r : r + 1, :]
    sums[...] = jnp.zeros_like(sums)

    def taps_of(source):
        return [source[pl.ds(SUB - 1 + b, ocol, stride=2), :].astype(BF16) for b in range(3)]

    carry2[...] = dot(jnp.concatenate(taps_of(up), axis=1), wf[3 * mid :, mid:])

    def conv_block(k, none):
        trow = (k * ob) // half
        total = [jnp.zeros((SUB, cout), F32) for c in range(tiles_c)]
        above = carry2[...]
        for part in range(ob // LINES):
            first = pl.multiple_of(k * BLOCK, BLOCK) + 2 * part * LINES
            lines = [
                jnp.concatenate(taps_of(red.at[first + 2 * i]) + taps_of(red.at[first + 2 * i + 1]), axis=1)
                for i in range(LINES)
            ]
            y = dot(jnp.concatenate(lines, axis=0), wf[...])
            later = y[:, mid:]
            now = y[:, :mid] + jnp.concatenate([above, later[: (LINES - 1) * ocol]], axis=0)
            above = later[(LINES - 1) * ocol :]
            act, slope = silu_pair(now)
            slope = slope.reshape(LINES, ocol, mid)
            at = pl.ds(pl.multiple_of(k * ob, ob) + part * LINES, LINES)
            s2[at] = slope.astype(s2.dtype)
            col2[at, :] = slope[:, 0, :]
            short = []
            for i in range(LINES):
                slo[part * LINES + i] = xv[first + 2 * i, :, : chan // 2].astype(F32)
                shi[part * LINES + i] = xv[first + 2 * i, :, chan // 2 :].astype(F32)
                short.append(
                    jnp.concatenate(
                        [
                            room.at[part * LINES + i][pl.ds(0, ocol, stride=2), :].astype(BF16)
                            for room in (slo, shi)
                        ],
                        axis=1,
                    )
                )
            act, slope = silu_pair(
                dot(jnp.concatenate([act.astype(BF16), jnp.concatenate(short, axis=0)], axis=1), wph[...])
            )
            slope = slope.reshape(LINES, ocol, cout)
            s3[at] = slope.astype(s3.dtype)
            col3[at, :] = slope[:, 0, :]
            cells = jnp.sum(act.reshape(LINES, tiles_c, half // SUB, SUB, cout), axis=(0, 2))
            for c in range(tiles_c):
                total[c] = total[c] + cells[c]
        carry2[...] = above
        for c in range(tiles_c):
            slot = trow * tiles_c + c
            sums[slot] = sums[slot] + total[c]
        return none

    lax.fori_loop(0, steps, conv_block, 0)

    ao, cls = ao_ref[...], cls_ref[...]
    embed = jnp.sum(sums[...], axis=1) * (1.0 / (half * half))
    high, low = split(embed)
    first = dot(jnp.concatenate([high, low], axis=0), ghigh[...])
    gates = first[:slots] + first[slots:] + dot(high, glow[...])
    tval = jnp.tanh(gates[:, :att])
    gval = sigm(gates[:, att:])
    score = jnp.sum(tval * gval * ao, axis=1, keepdims=True)
    value = jnp.sum(embed * cls, axis=1, keepdims=True)
    slot = lax.broadcasted_iota(jnp.int32, (slots, 128), 0)
    marks = jnp.zeros(slot.shape, jnp.int32)
    for r in range(tiles_r):
        for c in range(tiles_c):
            mark = jnp.broadcast_to(tissue_ref[r : r + 1, c : c + 1], slot.shape)
            marks = jnp.where(slot == r * tiles_c + c, mark, marks)
    live = marks[:, 0:1] > 0
    top = jnp.max(jnp.where(live, score, -1e30), axis=0, keepdims=True)
    weight = jnp.where(live, jnp.exp(score - top), 0.0)
    lane = lax.broadcasted_iota(jnp.int32, (1, 128), 1)
    payload = jnp.where(
        lane == 0, top,
        jnp.where(
            lane == 1, jnp.sum(weight, axis=0, keepdims=True), jnp.sum(weight * value, axis=0, keepdims=True)
        ),
    )
    mine1[...] = payload
    got1[0] = payload
    for k, device in enumerate(everyone):
        remote(mine1, got1.at[k + 1], xs1.at[0], xr1.at[0], device).start()
    every1 = got1.at[pl.ds(1, len(everyone))]
    arrival1 = remote(every1, every1, xs1.at[0], xr1.at[0], everyone[0])
    dtanh = ao * gval * (1.0 - tval * tval)
    dsigm = ao * tval * gval * (1.0 - gval)
    high, low = split(jnp.concatenate([dtanh, dsigm], axis=1))
    first = dot_t(jnp.concatenate([high, low], axis=0), ghigh[...])
    slant = first[:slots] + first[slots:] + dot_t(high, glow[...])
    arrival1.wait()
    every = got1[...]
    best = jnp.max(every, axis=0)[:, 0:1]
    factor = jnp.exp(every[:, :, 0:1] - best[None])
    both = jnp.sum(every * factor, axis=0)
    total = both[:, 1:2]
    prob = jnp.where(live, jnp.exp(score - best), 0.0) / total
    gap = value - both[:, 2:3] / total
    dembed = prob * (cls + gap * slant) * (1.0 / (half * half))
    dembed_ref[...] = dembed

    def spread_rows(tiles):
        return jnp.concatenate([jnp.broadcast_to(dembed[t : t + 1], (half, cout)) for t in tiles], axis=0)

    line = jnp.concatenate([s3[0].astype(F32) * spread_rows(range(tiles_c)),
                            col3[...] * spread_rows(range(0, tiles_r * tiles_c, tiles_c))], axis=0).astype(BF16)
    line = dot_t(line, wph[:mid, :]) * jnp.concatenate([s2[0].astype(F32), col2[...]], axis=0)
    edges2[...] = line.astype(BF16)
    copies2 = edge_copies(
        edges2, landed2, es2, er2,
        ((0, ocol, 0), (ocol, orow, ocol), (0, 2 * SUB, ocol + orow)),
        (shifted(sizes, 0, -1), shifted(sizes, -1, 0), shifted(sizes, -1, -1)),
    )
    for copy in copies2:
        copy.start()

    def spatial_back(k, none):
        at = pl.ds(pl.multiple_of(k * (piece // 2), (piece // 2)), (piece // 2))
        trow = (k * (piece // 2)) // half
        spread = jnp.concatenate(
            [jnp.broadcast_to(dembed_ref[pl.ds(trow * tiles_c + c, 1), :], (half, cout)) for c in range(tiles_c)],
            axis=0,
        )
        dpre = (s3[at].astype(F32) * spread[None]).astype(BF16).reshape((piece // 2) * ocol, cout)
        both = dot_t(dpre, wph[...])
        dsx[at, 0:ocol, :] = both[:, :mid].reshape((piece // 2), ocol, mid) * s2[at].astype(F32)
        for i in range(piece // 2):
            line = both[i * ocol : (i + 1) * ocol]
            for c in range(2):
                room = red.at[pl.multiple_of(k * piece, piece) + 2 * i + c]
                room[pl.ds(0, ocol, stride=2), :] = line[:, mid + c * (chan // 2) : mid + (c + 1) * (chan // 2)]
                room[pl.ds(1, ocol, stride=2), :] = jnp.zeros((ocol, mid), F32)
        return none

    lax.fori_loop(0, rows // piece, spatial_back, 0, unroll=True)
    for copy in copies2:
        copy.wait()
    below = jnp.where(lax.axis_index("space") < sizes[1] - 1, 1.0, 0.0)
    beside = jnp.where(lax.axis_index("head") < sizes[0] - 1, 1.0, 0.0)
    dsx[orow, 0:ocol, :] = landed2[0:ocol, :].astype(F32) * below
    dsx[orow, ocol:, :] = landed2[ocol + orow :, :].astype(F32)[:SUB] * (below * beside)
    left[0:orow, :] = landed2[ocol : ocol + orow, :].astype(F32) * beside
    for r in range(orow):
        dsx[r, ocol : ocol + 1, :] = left[r : r + 1, :]

    def pair(i):
        return jnp.concatenate([dsx[i, 0:ocol, :], dsx[i, 1 : ocol + 1, :]], axis=1).astype(BF16)

    carry3[...] = dot_t(pair(orow), wb[4 * mid :, :])
    total_ref[...] = jnp.zeros_like(total_ref)

    def reduced_back(step, none):
        k = rows // piece - 1 - step
        first = pl.multiple_of(k * piece, piece)
        y = dot_t(jnp.concatenate([pair(k * (piece // 2) + i) for i in range(piece // 2)], axis=0), wb[...])
        for i in range(piece // 2):
            at = slice(i * ocol, (i + 1) * ocol)
            below = carry3[...] if i == (piece // 2) - 1 else y[(i + 1) * ocol : (i + 2) * ocol, 4 * mid :]
            odd = y[at, 2 * mid : 4 * mid] + below
            for dj in range(2):
                side = slice(dj * mid, (dj + 1) * mid)
                drs[step % 2, 2 * i, pl.ds(dj, ocol, stride=2), :] = y[at, side]
                drs[step % 2, 2 * i + 1, pl.ds(dj, ocol, stride=2), :] = odd[:, side]
        carry3[...] = y[0:ocol, 4 * mid :]
        dred = (drs[step % 2] * s1[pl.ds(first, piece)].astype(F32)).astype(BF16)
        dinput = dot_t(dred.reshape(piece * cols, mid), wrh[...]).reshape(piece, cols, chan)
        total = jnp.zeros((SUB, chan), F32)
        for r in range(piece):
            value = dinput[r]
            if r % 2 == 0:
                value = value + jnp.concatenate([red[first + r, 0:cols, :], red[first + r + 1, 0:cols, :]], axis=1)
            out_ref[first + r] = value.astype(BF16)
            total = total + jnp.sum((value * xv[first + r].astype(F32)).reshape(cols // SUB, SUB, chan), axis=0)
        total_ref[...] += total
        return none

    lax.fori_loop(0, rows // piece, reduced_back, 0, unroll=True)

    part = jnp.sum(total_ref[...], axis=0, keepdims=True)
    lines = chan // 128
    part = jnp.concatenate([part[:, k * 128 : (k + 1) * 128] for k in range(lines)], axis=0)
    mine2[...] = part
    got2[0] = part
    for k, device in enumerate(everyone):
        remote(mine2, got2.at[k + 1], xs2.at[0], xr2.at[0], device).start()
    every2 = got2.at[pl.ds(1, len(everyone))]
    arrival2 = remote(every2, every2, xs2.at[0], xr2.at[0], everyone[0])
    arrival2.wait()
    part = jnp.sum(got2[...], axis=0)
    delta = delta_ref[...]
    ddelta = jnp.concatenate([part[k : k + 1] for k in range(lines)], axis=1) / (1.0 + delta)
    norm = jnp.sqrt(jnp.sum(ddelta * ddelta, axis=1, keepdims=True) * (1.0 / chan) + 1e-06)
    result = delta + (2 * dir_ref[...] - 1).astype(F32) * float(ALPHA) * ddelta / norm
    delta_out[...] = result.reshape(chan)


def leave_kernel(v_ref, out_ref, sem):
    n = sem.shape[0]
    size = v_ref.shape[0] // n
    copies = [
        pltpu.make_async_copy(v_ref.at[pl.ds(k * size, size)], out_ref.at[pl.ds(k * size, size)], sem.at[k])
        for k in range(n)
    ]
    for copy in copies:
        copy.start()
    for copy in copies:
        copy.wait()


def shards(
    features, stain_delta, tissue, reduce_weight, spatial_weight, expand_weight, shortcut_weight, attn_tanh, attn_sigm,
    attn_out, classifier, step_dir,
):
    rows, cols, chan = features.shape
    mid = reduce_weight.shape[1]
    cout = expand_weight.shape[1]
    att = attn_out.shape[0]
    tiles_r, tiles_c = tissue.shape
    slots = -(-tiles_r * tiles_c // SUB) * SUB
    orow, ocol = rows // 2, cols // 2
    sizes = tuple(lax.axis_size(axis) for axis in AXES)
    n = sizes[0] * sizes[1]
    steps = rows // BLOCK
    ob = BLOCK // 2
    vmem = pl.BlockSpec(memory_space=pltpu.VMEM)
    hbm = pl.BlockSpec(memory_space=pl.ANY)
    V, D = pltpu.VMEM, pltpu.SemaphoreType.DMA

    grad, new_delta = pl.pallas_call(
        functools.partial(whole_kernel, sizes),
        out_shape=(OUT_SPACE((rows, cols, chan), BF16), jax.ShapeDtypeStruct((chan,), F32)),
        in_specs=[hbm, vmem, vmem, vmem, vmem, vmem, vmem, vmem, hbm, hbm, vmem, vmem],
        out_specs=(vmem, vmem),
        scratch_shapes=[
            V((rows, cols, chan), BF16),
            V((rows, cols + SUB, mid), F32),
            V((rows, cols, mid), F32),
            V((orow, ocol, mid), F32),
            V((orow, ocol, cout), F32),
            V((orow + 1, ocol + SUB, mid), F32),
            V((2, BLOCK // 2, cols, mid), F32),
            V((ob, cols, chan // 2), F32),
            V((ob, cols, chan // 2), F32),
            V((chan, mid), BF16),
            V((mid + chan, cout), BF16),
            V((6 * mid, 2 * mid), BF16),
            V((6 * mid, 2 * mid), BF16),
            V((cout, 2 * att), F32),
            V((cout, 2 * att), BF16),
            V((cout, 2 * att), BF16),
            V((slots, SUB, cout), F32),
            V((orow, mid), F32),
            V((orow, cout), F32),
            V((ocol, mid), F32),
            V((ocol, 2 * mid), F32),
            V((1, cols, chan), BF16),
            V((rows, 2 * SUB, chan), BF16),
            V((cols + SUB, mid), F32),
            V((rows, mid), F32),
            V((cols + rows, mid), BF16),
            V((cols + rows + 2 * SUB, mid), BF16),
            V((ocol + orow, mid), BF16),
            V((ocol + orow + 2 * SUB, mid), BF16),
            V((1, 128), F32),
            V((n, 1, 128), F32),
            V((chan // 128, 128), F32),
            V((n, chan // 128, 128), F32),
            V((slots, cout), F32),
            V((SUB, chan), F32),
            D((steps,)),
            D((4,)),
            D((3,)),
            D((3,)),
            D((3,)),
            D((3,)),
            D((1,)),
            D((1,)),
            D((1,)),
            D((1,)),
        ],
        compiler_params=pltpu.CompilerParams(
            vmem_limit_bytes=52 * 1024 * 1024, collective_id=0, has_side_effects=True
        ),
        name="slide",
    )(
        features, stain_delta[None, :], step_dir[None, :], tissue, reduce_weight, spatial_weight, expand_weight,
        shortcut_weight, attn_tanh, attn_sigm, attn_out[None, :], classifier[None, :],
    )
    feature_grad = pl.pallas_call(
        leave_kernel,
        out_shape=jax.ShapeDtypeStruct((rows, cols, chan), BF16),
        in_specs=[vmem],
        out_specs=hbm,
        scratch_shapes=[D((4,))],
        compiler_params=pltpu.CompilerParams(vmem_limit_bytes=1024 * 1024),
        name="leave",
    )(grad)
    return (feature_grad, new_delta)


def OUT_SPACE(shape, dtype):
    return pltpu.VMEM(shape, dtype)


def solution(mesh):
    return jax.shard_map(
        shards,
        mesh=mesh,
        in_specs=(P("space", "head", None), P(), P("space", "head")) + (P(),) * 9,
        out_specs=(P("space", "head", None), P()),
        check_vma=False,
    )
```

```python
import functools

import jax
import jax.numpy as jnp
from jax import lax
from jax.experimental import pallas as pl
from jax.experimental.pallas import tpu as pltpu
from jax.sharding import PartitionSpec as P

TILE = 64
ALPHA = 1
BLOCK = 32
SUB = 8
PART = 8
LINES = 8
F32 = jnp.float32
BF16 = jnp.bfloat16
MESH = pl.DeviceIdType.MESH
AXES = ("head", "space")


def sigm(value):
    return 0.5 + 0.5 * jnp.tanh(0.5 * value)


def silu_pair(h):
    t = jnp.tanh(h)
    u = 1.0 + t
    act = h * u
    return act, u + act * (1.0 - t)


def dot(a, b):
    return jnp.dot(a, b, preferred_element_type=F32)


def dot_t(a, b):
    return lax.dot_general(a, b, (((1,), (1,)), ((), ())), preferred_element_type=F32)


def column(row, width):
    return jnp.transpose(jnp.broadcast_to(row, (width, row.shape[1])))


def split(value):
    high = value.astype(BF16)
    return high, (value - high.astype(F32)).astype(BF16)


def shifted(sizes, a, b):
    return (
        lax.rem(lax.axis_index(AXES[0]) + sizes[0] + a, sizes[0]),
        lax.rem(lax.axis_index(AXES[1]) + sizes[1] + b, sizes[1]),
    )


def others(sizes):
    return [shifted(sizes, a, b) for a in range(sizes[0]) for b in range(sizes[1]) if a + b > 0]


def remote(source, target, send, recv, device):
    return pltpu.make_async_remote_copy(
        src_ref=source, dst_ref=target, send_sem=send, recv_sem=recv, device_id=device, device_id_type=MESH
    )


def edge_copies(edges, landed, send, recv, spans, targets):
    return [
        remote(edges.at[pl.ds(source, size)], landed.at[pl.ds(place, size)], send.at[k], recv.at[k], targets[k])
        for k, (source, size, place) in enumerate(spans)
    ]


def whole_kernel(
    sizes, x_ref, delta_ref, dir_ref, tissue_ref, wr_ref, sp_ref, we_ref, ws_ref, at_ref, as_ref, ao_ref, cls_ref,
    out_ref, delta_out,
    xv, red, s1, s2, s3, dsx, drs, slo, shi, wrh, wph, wf, wb, gate, ghigh, glow, sums, col2, col3, carry2, carry3,
    rowbuf, colbuf, up, left, edges1, landed1, edges2, landed2, mine1, got1, mine2, got2, dembed_ref, total_ref,
    x_sem, in_sem, es1, er1, es2, er2, xs1, xr1, xs2, xr2,
):
    rows, cols, chan = xv.shape
    mid, cout = we_ref.shape
    orow, ocol = rows // 2, cols // 2
    half = TILE // 2
    tiles_r, tiles_c = tissue_ref.shape
    slots = sums.shape[0]
    steps = rows // BLOCK
    ob = BLOCK // 2
    piece = BLOCK // 2
    att = ao_ref.shape[1]
    everyone = others(sizes)

    row_in = pltpu.make_async_copy(x_ref.at[pl.ds(rows - 1, 1)], rowbuf, in_sem.at[0])
    col_in = pltpu.make_async_copy(x_ref.at[:, pl.ds(cols - 2 * SUB, 2 * SUB), :], colbuf, in_sem.at[1])
    row_in.start()
    col_in.start()

    def chunk(k):
        return pltpu.make_async_copy(
            x_ref.at[pl.ds(k * BLOCK, BLOCK)], xv.at[pl.ds(k * BLOCK, BLOCK)], x_sem.at[k]
        )

    for k in range(steps):
        chunk(k).start()
    gate_in = [
        pltpu.make_async_copy(ref, gate.at[:, pl.ds(k * att, att)], in_sem.at[2 + k])
        for k, ref in enumerate((at_ref, as_ref))
    ]
    for copy in gate_in:
        copy.start()

    barrier = pltpu.get_barrier_semaphore()
    for device in everyone:
        pl.semaphore_signal(barrier, inc=1, device_id=device, device_id_type=MESH)

    wide = column(0.5 + 0.5 * delta_ref[...], mid)
    wrh[...] = (wr_ref[...].astype(F32) * wide).astype(BF16)
    wph[:mid, :] = (we_ref[...].astype(F32) * 0.5).astype(BF16)
    for k in range(cout // mid):
        at = slice(k * mid, (k + 1) * mid)
        wph[mid:, at] = (ws_ref[:, at].astype(F32) * wide).astype(BF16)
    none = jnp.zeros((mid, mid), BF16)
    for b in range(3):
        tap = [(sp_ref[a, b].astype(F32) * 0.5).astype(BF16) for a in range(3)]
        at = slice(b * mid, (b + 1) * mid)
        under = slice((3 + b) * mid, (4 + b) * mid)
        wf[at, :mid] = tap[1]
        wf[at, mid:] = none
        wf[under, :mid] = tap[2]
        wf[under, mid:] = tap[0]
        for k, a in enumerate((1, 2, 0)):
            if b == 0:
                wb[(2 * k + 1) * mid : (2 * k + 2) * mid, mid:] = tap[a]
                wb[2 * k * mid : (2 * k + 1) * mid, mid:] = none
            else:
                wb[(2 * k + b - 1) * mid : (2 * k + b) * mid, :mid] = tap[a]

    def reduce_block(k):
        chunk(k).wait()
        for part in range(BLOCK // PART):
            at = pl.ds(k * BLOCK + part * PART, PART)
            act, slope = silu_pair(dot(xv[at].reshape(PART * cols, chan), wrh[...]))
            s1[at] = slope.reshape(PART, cols, mid).astype(s1.dtype)
            red[at, SUB:, :] = act.reshape(PART, cols, mid)

    reduce_block(0)
    row_in.wait()
    col_in.wait()
    col = colbuf[:, SUB:, :].astype(F32)[:, SUB - 1, :].astype(BF16)
    edge, _ = silu_pair(dot(jnp.concatenate([rowbuf[0], col], axis=0), wrh[...]))
    edges1[...] = edge.astype(BF16)
    copies1 = edge_copies(
        edges1, landed1, es1, er1,
        ((0, cols, 0), (cols, rows, cols), (cols - 2 * SUB, 2 * SUB, cols + rows)),
        (shifted(sizes, 0, 1), shifted(sizes, 1, 0), shifted(sizes, 1, 1)),
    )
    pl.semaphore_wait(barrier, len(everyone))
    for copy in copies1:
        copy.start()
    for k in range(1, steps):
        reduce_block(k)
    for copy in gate_in:
        copy.wait()
    high, low = split(gate[...])
    ghigh[...] = high
    glow[...] = low
    for copy in copies1:
        copy.wait()
    above = jnp.where(lax.axis_index("space") > 0, 1.0, 0.0)
    beside = jnp.where(lax.axis_index("head") > 0, 1.0, 0.0)
    up[0:SUB, :] = landed1[cols + rows :, :].astype(F32)[SUB:] * (above * beside)
    up[SUB:, :] = landed1[0:cols, :].astype(F32) * above
    left[...] = landed1[cols : cols + rows, :].astype(F32) * beside
    for r in range(rows):
        red[r, SUB - 1 : SUB, :] = left[r : r + 1, :]
    sums[...] = jnp.zeros_like(sums)

    def taps_of(source):
        return [source[pl.ds(SUB - 1 + b, ocol, stride=2), :].astype(BF16) for b in range(3)]

    carry2[...] = dot(jnp.concatenate(taps_of(up), axis=1), wf[3 * mid :, mid:])

    def conv_block(k, none):
        trow = (k * ob) // half
        total = [jnp.zeros((SUB, cout), F32) for c in range(tiles_c)]
        above = carry2[...]
        for part in range(ob // LINES):
            first = pl.multiple_of(k * BLOCK, BLOCK) + 2 * part * LINES
            lines = [
                jnp.concatenate(taps_of(red.at[first + 2 * i]) + taps_of(red.at[first + 2 * i + 1]), axis=1)
                for i in range(LINES)
            ]
            y = dot(jnp.concatenate(lines, axis=0), wf[...])
            later = y[:, mid:]
            now = y[:, :mid] + jnp.concatenate([above, later[: (LINES - 1) * ocol]], axis=0)
            above = later[(LINES - 1) * ocol :]
            act, slope = silu_pair(now)
            slope = slope.reshape(LINES, ocol, mid)
            at = pl.ds(pl.multiple_of(k * ob, ob) + part * LINES, LINES)
            s2[at] = slope.astype(s2.dtype)
            col2[at, :] = slope[:, 0, :]
            short = []
            for i in range(LINES):
                slo[part * LINES + i] = xv[first + 2 * i, :, : chan // 2].astype(F32)
                shi[part * LINES + i] = xv[first + 2 * i, :, chan // 2 :].astype(F32)
                short.append(
                    jnp.concatenate(
                        [
                            room.at[part * LINES + i][pl.ds(0, ocol, stride=2), :].astype(BF16)
                            for room in (slo, shi)
                        ],
                        axis=1,
                    )
                )
            act, slope = silu_pair(
                dot(jnp.concatenate([act.astype(BF16), jnp.concatenate(short, axis=0)], axis=1), wph[...])
            )
            slope = slope.reshape(LINES, ocol, cout)
            s3[at] = slope.astype(s3.dtype)
            col3[at, :] = slope[:, 0, :]
            cells = jnp.sum(act.reshape(LINES, tiles_c, half // SUB, SUB, cout), axis=(0, 2))
            for c in range(tiles_c):
                total[c] = total[c] + cells[c]
        carry2[...] = above
        for c in range(tiles_c):
            slot = trow * tiles_c + c
            sums[slot] = sums[slot] + total[c]
        return none

    lax.fori_loop(0, steps, conv_block, 0, unroll=2)

    ao, cls = ao_ref[...], cls_ref[...]
    embed = jnp.sum(sums[...], axis=1) * (1.0 / (half * half))
    high, low = split(embed)
    first = dot(jnp.concatenate([high, low], axis=0), ghigh[...])
    gates = first[:slots] + first[slots:] + dot(high, glow[...])
    tval = jnp.tanh(gates[:, :att])
    gval = sigm(gates[:, att:])
    score = jnp.sum(tval * gval * ao, axis=1, keepdims=True)
    value = jnp.sum(embed * cls, axis=1, keepdims=True)
    slot = lax.broadcasted_iota(jnp.int32, (slots, 128), 0)
    marks = jnp.zeros(slot.shape, jnp.int32)
    for r in range(tiles_r):
        for c in range(tiles_c):
            mark = jnp.broadcast_to(tissue_ref[r : r + 1, c : c + 1], slot.shape)
            marks = jnp.where(slot == r * tiles_c + c, mark, marks)
    live = marks[:, 0:1] > 0
    top = jnp.max(jnp.where(live, score, -1e30), axis=0, keepdims=True)
    weight = jnp.where(live, jnp.exp(score - top), 0.0)
    lane = lax.broadcasted_iota(jnp.int32, (1, 128), 1)
    payload = jnp.where(
        lane == 0, top,
        jnp.where(
            lane == 1, jnp.sum(weight, axis=0, keepdims=True), jnp.sum(weight * value, axis=0, keepdims=True)
        ),
    )
    mine1[...] = payload
    got1[0] = payload
    for k, device in enumerate(everyone):
        remote(mine1, got1.at[k + 1], xs1.at[0], xr1.at[0], device).start()
    every1 = got1.at[pl.ds(1, len(everyone))]
    arrival1 = remote(every1, every1, xs1.at[0], xr1.at[0], everyone[0])
    dtanh = ao * gval * (1.0 - tval * tval)
    dsigm = ao * tval * gval * (1.0 - gval)
    high, low = split(jnp.concatenate([dtanh, dsigm], axis=1))
    first = dot_t(jnp.concatenate([high, low], axis=0), ghigh[...])
    slant = first[:slots] + first[slots:] + dot_t(high, glow[...])
    arrival1.wait()
    every = got1[...]
    best = jnp.max(every, axis=0)[:, 0:1]
    factor = jnp.exp(every[:, :, 0:1] - best[None])
    both = jnp.sum(every * factor, axis=0)
    total = both[:, 1:2]
    prob = jnp.where(live, jnp.exp(score - best), 0.0) / total
    gap = value - both[:, 2:3] / total
    dembed = prob * (cls + gap * slant) * (1.0 / (half * half))
    dembed_ref[...] = dembed

    def spread_rows(tiles):
        return jnp.concatenate([jnp.broadcast_to(dembed[t : t + 1], (half, cout)) for t in tiles], axis=0)

    line = jnp.concatenate([s3[0].astype(F32) * spread_rows(range(tiles_c)),
                            col3[...] * spread_rows(range(0, tiles_r * tiles_c, tiles_c))], axis=0).astype(BF16)
    line = dot_t(line, wph[:mid, :]) * jnp.concatenate([s2[0].astype(F32), col2[...]], axis=0)
    edges2[...] = line.astype(BF16)
    copies2 = edge_copies(
        edges2, landed2, es2, er2,
        ((0, ocol, 0), (ocol, orow, ocol), (0, 2 * SUB, ocol + orow)),
        (shifted(sizes, 0, -1), shifted(sizes, -1, 0), shifted(sizes, -1, -1)),
    )
    for copy in copies2:
        copy.start()

    def spatial_back(k, none):
        at = pl.ds(pl.multiple_of(k * (piece // 2), (piece // 2)), (piece // 2))
        trow = (k * (piece // 2)) // half
        spread = jnp.concatenate(
            [jnp.broadcast_to(dembed_ref[pl.ds(trow * tiles_c + c, 1), :], (half, cout)) for c in range(tiles_c)],
            axis=0,
        )
        dpre = (s3[at].astype(F32) * spread[None]).astype(BF16).reshape((piece // 2) * ocol, cout)
        both = dot_t(dpre, wph[...])
        dsx[at, 0:ocol, :] = both[:, :mid].reshape((piece // 2), ocol, mid) * s2[at].astype(F32)
        for i in range(piece // 2):
            line = both[i * ocol : (i + 1) * ocol]
            for c in range(2):
                room = red.at[pl.multiple_of(k * piece, piece) + 2 * i + c]
                room[pl.ds(0, ocol, stride=2), :] = line[:, mid + c * (chan // 2) : mid + (c + 1) * (chan // 2)]
                room[pl.ds(1, ocol, stride=2), :] = jnp.zeros((ocol, mid), F32)
        return none

    lax.fori_loop(0, rows // piece, spatial_back, 0, unroll=True)
    for copy in copies2:
        copy.wait()
    below = jnp.where(lax.axis_index("space") < sizes[1] - 1, 1.0, 0.0)
    beside = jnp.where(lax.axis_index("head") < sizes[0] - 1, 1.0, 0.0)
    dsx[orow, 0:ocol, :] = landed2[0:ocol, :].astype(F32) * below
    dsx[orow, ocol:, :] = landed2[ocol + orow :, :].astype(F32)[:SUB] * (below * beside)
    left[0:orow, :] = landed2[ocol : ocol + orow, :].astype(F32) * beside
    for r in range(orow):
        dsx[r, ocol : ocol + 1, :] = left[r : r + 1, :]

    def pair(i):
        return jnp.concatenate([dsx[i, 0:ocol, :], dsx[i, 1 : ocol + 1, :]], axis=1).astype(BF16)

    carry3[...] = dot_t(pair(orow), wb[4 * mid :, :])
    total_ref[...] = jnp.zeros_like(total_ref)

    def reduced_back(step, none):
        k = rows // piece - 1 - step
        first = pl.multiple_of(k * piece, piece)
        y = dot_t(jnp.concatenate([pair(k * (piece // 2) + i) for i in range(piece // 2)], axis=0), wb[...])
        for i in range(piece // 2):
            at = slice(i * ocol, (i + 1) * ocol)
            below = carry3[...] if i == (piece // 2) - 1 else y[(i + 1) * ocol : (i + 2) * ocol, 4 * mid :]
            odd = y[at, 2 * mid : 4 * mid] + below
            for dj in range(2):
                side = slice(dj * mid, (dj + 1) * mid)
                drs[step % 2, 2 * i, pl.ds(dj, ocol, stride=2), :] = y[at, side]
                drs[step % 2, 2 * i + 1, pl.ds(dj, ocol, stride=2), :] = odd[:, side]
        carry3[...] = y[0:ocol, 4 * mid :]
        dred = (drs[step % 2] * s1[pl.ds(first, piece)].astype(F32)).astype(BF16)
        dinput = dot_t(dred.reshape(piece * cols, mid), wrh[...]).reshape(piece, cols, chan)
        total = jnp.zeros((SUB, chan), F32)
        for r in range(piece):
            value = dinput[r]
            if r % 2 == 0:
                value = value + jnp.concatenate([red[first + r, 0:cols, :], red[first + r + 1, 0:cols, :]], axis=1)
            out_ref[first + r] = value.astype(BF16)
            total = total + jnp.sum((value * xv[first + r].astype(F32)).reshape(cols // SUB, SUB, chan), axis=0)
        total_ref[...] += total
        return none

    lax.fori_loop(0, rows // piece, reduced_back, 0, unroll=True)

    part = jnp.sum(total_ref[...], axis=0, keepdims=True)
    lines = chan // 128
    part = jnp.concatenate([part[:, k * 128 : (k + 1) * 128] for k in range(lines)], axis=0)
    mine2[...] = part
    got2[0] = part
    for k, device in enumerate(everyone):
        remote(mine2, got2.at[k + 1], xs2.at[0], xr2.at[0], device).start()
    every2 = got2.at[pl.ds(1, len(everyone))]
    arrival2 = remote(every2, every2, xs2.at[0], xr2.at[0], everyone[0])
    arrival2.wait()
    part = jnp.sum(got2[...], axis=0)
    delta = delta_ref[...]
    ddelta = jnp.concatenate([part[k : k + 1] for k in range(lines)], axis=1) / (1.0 + delta)
    norm = jnp.sqrt(jnp.sum(ddelta * ddelta, axis=1, keepdims=True) * (1.0 / chan) + 1e-06)
    result = delta + (2 * dir_ref[...] - 1).astype(F32) * float(ALPHA) * ddelta / norm
    delta_out[...] = result.reshape(chan)


def leave_kernel(v_ref, out_ref, sem):
    n = sem.shape[0]
    size = v_ref.shape[0] // n
    copies = [
        pltpu.make_async_copy(v_ref.at[pl.ds(k * size, size)], out_ref.at[pl.ds(k * size, size)], sem.at[k])
        for k in range(n)
    ]
    for copy in copies:
        copy.start()
    for copy in copies:
        copy.wait()


def shards(
    features, stain_delta, tissue, reduce_weight, spatial_weight, expand_weight, shortcut_weight, attn_tanh, attn_sigm,
    attn_out, classifier, step_dir,
):
    rows, cols, chan = features.shape
    mid = reduce_weight.shape[1]
    cout = expand_weight.shape[1]
    att = attn_out.shape[0]
    tiles_r, tiles_c = tissue.shape
    slots = -(-tiles_r * tiles_c // SUB) * SUB
    orow, ocol = rows // 2, cols // 2
    sizes = tuple(lax.axis_size(axis) for axis in AXES)
    n = sizes[0] * sizes[1]
    steps = rows // BLOCK
    ob = BLOCK // 2
    vmem = pl.BlockSpec(memory_space=pltpu.VMEM)
    hbm = pl.BlockSpec(memory_space=pl.ANY)
    V, D = pltpu.VMEM, pltpu.SemaphoreType.DMA

    grad, new_delta = pl.pallas_call(
        functools.partial(whole_kernel, sizes),
        out_shape=(OUT_SPACE((rows, cols, chan), BF16), jax.ShapeDtypeStruct((chan,), F32)),
        in_specs=[hbm, vmem, vmem, vmem, vmem, vmem, vmem, vmem, hbm, hbm, vmem, vmem],
        out_specs=(vmem, vmem),
        scratch_shapes=[
            V((rows, cols, chan), BF16),
            V((rows, cols + SUB, mid), F32),
            V((rows, cols, mid), F32),
            V((orow, ocol, mid), F32),
            V((orow, ocol, cout), F32),
            V((orow + 1, ocol + SUB, mid), F32),
            V((2, BLOCK // 2, cols, mid), F32),
            V((ob, cols, chan // 2), F32),
            V((ob, cols, chan // 2), F32),
            V((chan, mid), BF16),
            V((mid + chan, cout), BF16),
            V((6 * mid, 2 * mid), BF16),
            V((6 * mid, 2 * mid), BF16),
            V((cout, 2 * att), F32),
            V((cout, 2 * att), BF16),
            V((cout, 2 * att), BF16),
            V((slots, SUB, cout), F32),
            V((orow, mid), F32),
            V((orow, cout), F32),
            V((ocol, mid), F32),
            V((ocol, 2 * mid), F32),
            V((1, cols, chan), BF16),
            V((rows, 2 * SUB, chan), BF16),
            V((cols + SUB, mid), F32),
            V((rows, mid), F32),
            V((cols + rows, mid), BF16),
            V((cols + rows + 2 * SUB, mid), BF16),
            V((ocol + orow, mid), BF16),
            V((ocol + orow + 2 * SUB, mid), BF16),
            V((1, 128), F32),
            V((n, 1, 128), F32),
            V((chan // 128, 128), F32),
            V((n, chan // 128, 128), F32),
            V((slots, cout), F32),
            V((SUB, chan), F32),
            D((steps,)),
            D((4,)),
            D((3,)),
            D((3,)),
            D((3,)),
            D((3,)),
            D((1,)),
            D((1,)),
            D((1,)),
            D((1,)),
        ],
        compiler_params=pltpu.CompilerParams(
            vmem_limit_bytes=52 * 1024 * 1024, collective_id=0, has_side_effects=True
        ),
        name="slide",
    )(
        features, stain_delta[None, :], step_dir[None, :], tissue, reduce_weight, spatial_weight, expand_weight,
        shortcut_weight, attn_tanh, attn_sigm, attn_out[None, :], classifier[None, :],
    )
    feature_grad = pl.pallas_call(
        leave_kernel,
        out_shape=jax.ShapeDtypeStruct((rows, cols, chan), BF16),
        in_specs=[vmem],
        out_specs=hbm,
        scratch_shapes=[D((4,))],
        compiler_params=pltpu.CompilerParams(vmem_limit_bytes=1024 * 1024),
        name="leave",
    )(grad)
    return (feature_grad, new_delta)


def OUT_SPACE(shape, dtype):
    return pltpu.VMEM(shape, dtype)


def solution(mesh):
    return jax.shard_map(
        shards,
        mesh=mesh,
        in_specs=(P("space", "head", None), P(), P("space", "head")) + (P(),) * 9,
        out_specs=(P("space", "head", None), P()),
        check_vma=False,
    )
```
